128 devices in a mesh: sec: 4 (over y), row: 8 (over x, core), col: 4 (over z).
Axes of the slice: x: 4, y: 4, z: 4, core: 2. Of those that a mesh axis runs over, the one named last changes fastest.
Arguments:
- child_inv: bfloat16 [4, 4096, 4096], P('sec', 'col', 'row'), as said below
- child_low: bfloat16 [4, 2048, 4096], P('sec', 'row', 'col'), may hold values from -0.09375 to 0.09375
- parent_inv: bfloat16 [4, 6144, 3072], P('sec', 'col', 'row'), as said below
- parent_low: bfloat16 [4, 2048, 3072], P('sec', 'row', 'col'), may hold values from -0.078125 to 0.078125
- root_inv: bfloat16 [12288, 12288], P('col', ('sec', 'row')), as said below
- child_map: int32 [4, 2048], replicated, may hold values from 0 to 8191, as said below
- parent_map: int32 [2, 2048], replicated, may hold values from 0 to 12287, as said below
- child_rhs: float32 [4, 4096, 512], P('sec', 'row', 'col'), may hold values from -6 to 6
- parent_rhs: float32 [4, 3072, 512], P('sec', 'row', 'col'), may hold values from -6 to 6
- root_rhs: float32 [12288, 512], P(('sec', 'row'), 'col'), may hold values from -6 to 6
- child_back: float32 [4, 4096, 512], P('sec', 'col', 'row'), may hold values from -6 to 6
- parent_back: float32 [4, 3072, 512], P('sec', 'col', 'row'), may hold values from -6 to 6
- root_back: float32 [4, 3072, 512], P('col', ('sec', 'row')), may hold values from -6 to 6
Outputs:
- child_up: float32 [4, 4096, 512], P('sec', 'col', 'row')
- parent_up: float32 [4, 3072, 512], P('sec', 'col', 'row')
- root_up: float32 [4, 3072, 512], P('col', ('sec', 'row'))
- child_x: float32 [4, 4096, 512], P('sec', 'row', 'col')
- parent_x: float32 [4, 3072, 512], P('sec', 'row', 'col')
- root_x: float32 [12288, 512], P(('sec', 'row'), 'col')
The draws below stay inside these ranges and needn't reach their ends.
Inputs may be any that keep to these rules, and one draw needn't show every extreme that they name: `child_inv`: zero above the diagonal of each child pivot block. `parent_inv`: the two halves side by side are zero above the diagonal. `root_inv`: zero above the diagonal. `child_map`: entries of one row are distinct; row s points into the front of parent s // 2. `parent_map`: entries of one row are distinct.
All inputs are finite; a program needn't handle non-finite values.
Results may differ from the reference program's by a relative error of at most 0.014.
Values may be sent and summed in bfloat16 or wider, within the bound.
A program may use at most 64 MiB of HBM per device.

```python
import jax
import jax.numpy as jnp

P1 = 4096
C1 = 2048
P2 = 6144
C2 = 2048
P3 = 12288
FW = 512
BW = 512
SECTIONS = 4
COL_BLOCKS = 4
N_COL = 4


def lower_factor(key, members, order):
    base = jax.random.normal(key, (members, order, order), jnp.float32)
    return jnp.tril(base) / jnp.sqrt(order * 1.0) + jnp.eye(order, dtype=jnp.float32)


def spread_map(key, members, length, extent):
    result_rows = []
    for member in range(members):
        member_key = jax.random.fold_in(key, member)
        middle = jax.random.permutation(jax.random.fold_in(member_key, 1), extent - 2)[:length - 2] + 1
        picked = jnp.concatenate([jnp.array([0, extent - 1], jnp.int32), middle.astype(jnp.int32)])
        result_rows.append(jax.random.permutation(jax.random.fold_in(member_key, 2), picked))
    return jnp.stack(result_rows).astype(jnp.int32)


def draw_child_inv(key, part):
    return lower_factor(jax.random.fold_in(key, 11), SECTIONS, P1).astype(jnp.bfloat16)


def draw_parent_inv(key, part):
    whole = lower_factor(jax.random.fold_in(key, 12), 2, P2)
    return whole.reshape(2, P2, 2, P2 // 2).transpose(0, 2, 1, 3).reshape(4, P2, P2 // 2).astype(jnp.bfloat16)


def draw_root_inv(key, part):
    return lower_factor(jax.random.fold_in(key, 13), 1, P3)[0].astype(jnp.bfloat16)


def draw_child_map(key, part):
    return spread_map(jax.random.fold_in(key, 21), SECTIONS, C1, P2 + C2)


def draw_parent_map(key, part):
    return spread_map(jax.random.fold_in(key, 22), 2, C2, P3)


def level_of(rng, shape, shards, smallest, high):
    gain = 1.0
    for position, parts in shards:
        heights = jax.random.uniform(jax.random.fold_in(jax.random.fold_in(rng, 6), position), (parts,), jnp.float32, smallest / len(shards), high / len(shards))
        gain = gain * jnp.repeat(jnp.exp(heights), shape[position] // parts).reshape((-1,) + (1,) * (len(shape) - 1 - position))
    return gain


def gaussian(rng, shape, scale, limit, shards=(), held_as=jnp.bfloat16):
    gain = level_of(rng, shape, shards, -0.22, 0.18) if shards else 1.0
    values = jax.random.normal(rng, shape, jnp.float32) * scale * gain
    return jnp.minimum(jnp.maximum(values, -limit), limit).astype(held_as)


def setup_inputs(seed: int = 0) -> dict:
    key_of = jax.random.split(jax.random.key(seed), 14)
    return {
        "child_inv": draw_child_inv(jax.random.fold_in(key_of[13], 71), 0),
        "child_low": gaussian(key_of[1], (SECTIONS, C1, P1), P1 ** -0.5, 0.09375, ((0, 4), (1, 8), (2, 4))),
        "parent_inv": draw_parent_inv(jax.random.fold_in(key_of[13], 71), 0),
        "parent_low": gaussian(key_of[3], (SECTIONS, C2, P2 // 2), P2 ** -0.5, 0.078125, ((0, 4), (1, 8), (2, 4))),
        "root_inv": draw_root_inv(jax.random.fold_in(key_of[13], 71), 0),
        "child_map": draw_child_map(jax.random.fold_in(key_of[13], 71), 0),
        "parent_map": draw_parent_map(jax.random.fold_in(key_of[13], 71), 0),
        "child_rhs": gaussian(key_of[7], (SECTIONS, P1, FW), 1.0, 6.0, ((0, 4), (1, 8), (2, 4)), jnp.float32),
        "parent_rhs": gaussian(key_of[8], (SECTIONS, P2 // 2, FW), 1.0, 6.0, ((0, 4), (1, 8), (2, 4)), jnp.float32),
        "root_rhs": gaussian(key_of[9], (P3, FW), 1.0, 6.0, ((0, 32), (1, 4)), jnp.float32),
        "child_back": gaussian(key_of[10], (SECTIONS, P1, BW), 1.0, 6.0, ((0, 4), (1, 4), (2, 8)), jnp.float32),
        "parent_back": gaussian(key_of[11], (SECTIONS, P2 // 2, BW), 1.0, 6.0, ((0, 4), (1, 4), (2, 8)), jnp.float32),
        "root_back": gaussian(key_of[12], (COL_BLOCKS, P3 // COL_BLOCKS, BW), 1.0, 6.0, ((0, 4), (1, 32)), jnp.float32),
    }


def product(left, right):
    return jnp.dot(left, right.astype(jnp.bfloat16), preferred_element_type=jnp.float32)


def reference(child_inv, child_low, parent_inv, parent_low, root_inv, child_map, parent_map, child_rhs, parent_rhs, root_rhs, child_back, parent_back, root_back):
    quota = P2 // (2 * N_COL)
    child_up = jnp.stack([product(child_inv[member], child_rhs[member]) for member in range(4)])
    contrib = [-product(child_low[member], child_up[member]) for member in range(4)]
    pivot_rhs = parent_rhs.reshape(2, P2, FW)
    pivot_back = parent_back.reshape(2, 2, N_COL, quota, BW).transpose(0, 2, 1, 3, 4).reshape(2, P2, BW)
    inverses = []
    couplings = []
    solved = []
    updates = []
    for parent in range(2):
        inverse = jnp.concatenate([parent_inv[2 * parent], parent_inv[2 * parent + 1]], axis=1)
        coupling = parent_low[2 * parent:2 * parent + 2].reshape(2, C2, N_COL, quota).transpose(1, 2, 0, 3).reshape(C2, P2)
        front = jnp.zeros((P2 + C2, FW), jnp.float32)
        front = front.at[child_map[2 * parent]].add(contrib[2 * parent])
        front = front.at[child_map[2 * parent + 1]].add(contrib[2 * parent + 1])
        upward = product(inverse, pivot_rhs[parent] + front[:P2])
        updates.append(front[P2:] - product(coupling, upward))
        inverses.append(inverse)
        couplings.append(coupling)
        solved.append(upward)
    parent_up = jnp.stack(solved).reshape(2, N_COL, 2, quota, FW).transpose(0, 2, 1, 3, 4).reshape(4, P2 // 2, FW)
    root_front = jnp.zeros((P3, FW), jnp.float32)
    root_front = root_front.at[parent_map[0]].add(updates[0])
    root_front = root_front.at[parent_map[1]].add(updates[1])
    root_up = product(root_inv, root_rhs + root_front).reshape(N_COL, P3 // N_COL, FW)
    root_x = product(root_inv.T, root_back.reshape(P3, BW))
    root_bf = root_x.astype(jnp.bfloat16)
    parent_rows = []
    fronts = []
    for parent in range(2):
        picked = root_bf[parent_map[parent]]
        residue = pivot_back[parent] - jnp.dot(couplings[parent].T, picked, preferred_element_type=jnp.float32)
        solution = product(inverses[parent].T, residue)
        parent_rows.append(solution)
        fronts.append(jnp.concatenate([solution.astype(jnp.bfloat16), picked], axis=0))
    parent_x = jnp.stack(parent_rows).reshape(4, P2 // 2, BW)
    child_rows = []
    for member in range(4):
        chosen = fronts[member // 2][child_map[member]]
        residue = child_back[member] - jnp.dot(child_low[member].T, chosen, preferred_element_type=jnp.float32)
        child_rows.append(product(child_inv[member].T, residue))
    child_x = jnp.stack(child_rows)
    return child_up, parent_up, root_up, child_x, parent_x, root_x
```

```python
import types

import jax
import jax.numpy as jnp
from jax import lax
from jax.experimental import pallas as pl
from jax.experimental.pallas import tpu as pltpu
from jax.sharding import PartitionSpec as P

BF = jnp.bfloat16
F32 = jnp.float32
I32 = jnp.int32
MESH = pl.DeviceIdType.MESH

INPUTS = dict(
    wci=((1024, 512), BF),
    wcl=((256, 1024), BF),
    wpi=((1536, 384), BF),
    wpl=((256, 768), BF),
    wr=((3072, 384), BF),
    cmap=((4, 2048), I32),
    pmap=((2, 2048), I32),
    i_cr=((512, 128), F32),
    i_pr=((384, 128), F32),
    i_rr=((384, 128), F32),
    i_cb=((64, 1024), F32),
    i_pb=((64, 768), F32),
    i_rb=((96, 512), F32),
)
OUTPUTS = dict(
    o_cu=((64, 1024), F32),
    o_pu=((64, 768), F32),
    o_ru=((96, 512), F32),
    o_cx=((512, 128), F32),
    o_px=((384, 128), F32),
    o_rx=((384, 128), F32),
)
SCRATCH = dict(
    sel=((512, 4096), BF),
    rsel=((384, 4096), BF),
    f_x=((4, 512, 128), BF),
    f_ps=((4, 512, 128), BF),
    f_pr=((4, 512, 128), BF),
    f_xs=((3, 512, 128), BF),
    f_xr=((3, 512, 128), BF),
    f_u=((512, 128), F32),
    f_us=((512, 128), F32),
    f_x2=((4, 2, 512, 128), BF),
    f_cs=((3, 256, 128), BF),
    f_cr=((3, 256, 128), BF),
    f_c=((2, 8, 256, 128), BF),
    f_fc=((128, 128), F32),
    f_px=((4, 384, 128), BF),
    f_qs=((4, 768, 128), BF),
    f_k=((4, 768, 128), F32),
    f_qr=((4, 768, 128), BF),
    f_qxs=((3, 768, 128), BF),
    f_qxr=((3, 768, 128), BF),
    f_q=((768, 128), F32),
    f_qps=((384, 128), BF),
    f_qpr=((384, 128), BF),
    f_pu=((384, 128), F32),
    f_pus=((384, 128), F32),
    f_x3=((4, 2, 384, 128), BF),
    f_ds=((3, 256, 128), BF),
    f_dr=((3, 256, 128), BF),
    f_up=((2, 128, 128), F32),
    f_ups=((128, 128), BF),
    f_upr=((128, 128), BF),
    f_r=((2, 8, 2, 128, 128), BF),
    f_rx=((4, 384, 128), BF),
    f_t=((2, 4, 4, 96, 512), BF),
    f_tr=((4, 4, 96, 512), BF),
    f_as=((3, 4, 96, 256), BF),
    f_bs=((3, 4, 96, 256), BF),
    f_ar=((3, 4, 96, 256), BF),
    f_br=((3, 4, 96, 256), BF),
    f_oa=((4, 96, 256), F32),
    f_ob=((4, 96, 256), F32),
    f_a2s=((3, 96, 256), BF),
    f_b2s=((3, 96, 256), BF),
    f_a2r=((3, 96, 256), BF),
    f_b2r=((3, 96, 256), BF),
    b_y=((4, 4, 2, 96, 512), BF),
    b_r=((4, 384, 128), F32),
    b_rs=((3, 384, 128), BF),
    b_rr=((3, 384, 128), BF),
    b_rx=((384, 128), BF),
    b_t=((2, 4, 2, 256, 128), BF),
    b_tr=((2, 4, 256, 128), BF),
    b_txs=((3, 2, 256, 128), BF),
    b_txr=((3, 2, 256, 128), BF),
    b_tp=((2, 256, 128), BF),
    b_tpr=((3, 256, 128), BF),
    b_pk=((4, 256, 128), BF),
    b_es=((4, 384, 128), BF),
    b_er=((4, 384, 128), BF),
    b_exs=((3, 384, 128), BF),
    b_exr=((3, 384, 128), BF),
    b_pbs=((64, 768), F32),
    b_g=((4, 2, 2, 384, 128), BF),
    b_hs=((3, 384, 128), BF),
    b_hr=((3, 384, 128), BF),
    b_fx=((512, 128), BF),
    b_v=((2, 4, 2, 256, 128), BF),
    b_vr=((2, 4, 256, 128), BF),
    b_vxs=((3, 2, 256, 128), BF),
    b_vxr=((3, 2, 256, 128), BF),
    b_vp=((2, 256, 128), BF),
    b_vpr=((256, 128), BF),
    b_ck=((4, 256, 128), BF),
    b_ls=((4, 512, 128), BF),
    b_k=((4, 512, 128), F32),
    b_lr=((4, 512, 128), BF),
    b_lxs=((3, 512, 128), BF),
    b_lxr=((3, 512, 128), BF),
    b_cbs=((64, 1024), F32),
    b_h=((4, 2, 512, 128), BF),
    b_ms=((3, 512, 128), BF),
    b_mr=((3, 512, 128), BF),
)
N_REMOTE = 180
N_LOCAL = len(INPUTS) + len(OUTPUTS)


def dot(a, b):
    return jnp.dot(a, b, preferred_element_type=F32)


def dot_t(a, b):
    return lax.dot_general(a, b, (((0,), (0,)), ((), ())), preferred_element_type=F32)


def body(*refs):
    n_in, n_out = len(INPUTS), len(OUTPUTS)
    hbm_in = refs[:n_in]
    hbm_out = refs[n_in : n_in + n_out]
    rest = refs[n_in + n_out :]
    names = [*INPUTS, *OUTPUTS, *SCRATCH]
    v = types.SimpleNamespace(**dict(zip(names, rest)))
    send_sems, recv_sems, local_sems = rest[len(names) :]

    sec = lax.axis_index("sec")
    row = lax.axis_index("row")
    z = lax.axis_index("col")
    x = row // 2
    c = row % 2
    sib = 1 - c
    h = sec % 2
    p = sec // 2
    oh = 1 - h

    def at_x(d):
        return {"row": ((x + d) % 4) * 2 + c}

    def at_y(d):
        return {"sec": (sec + d) % 4}

    def at_z(d):
        return {"col": (z + d) % 4}

    sibling = {"row": x * 2 + sib}
    pair = {"sec": p * 2 + oh}

    loads = {}
    for i, (ref, src) in enumerate(zip(rest, hbm_in)):
        if len(src.shape) > len(ref.shape):
            src = src.at[0]
        loads[id(ref)] = pltpu.make_async_copy(src, ref, local_sems.at[i])
    first = (v.i_rb, v.i_cr, v.i_cb, v.i_pb, v.wci, v.wr, v.cmap, v.pmap)
    for ref in first + (v.wcl, v.i_pr, v.wpi, v.wpl, v.i_rr):
        loads[id(ref)].start()

    def need(*wanted):
        for ref in wanted:
            copy = loads.pop(id(ref), None)
            if copy is not None:
                copy.wait()

    stores = []

    def emit(ref, i):
        dst = hbm_out[i]
        if len(dst.shape) > 2:
            dst = dst.at[0]
        copy = pltpu.make_async_copy(ref, dst, local_sems.at[n_in + i])
        copy.start()
        stores.append(copy)

    barrier = pltpu.get_barrier_semaphore()
    peers = [sibling] + [f(d) for f in (at_x, at_y, at_z) for d in (1, 2, 3)]
    for peer in peers:
        pl.semaphore_signal(barrier, inc=1, device_id=peer, device_id_type=MESH)
    pl.semaphore_wait(barrier, len(peers))

    sent = []

    def send(src, dst, peer):
        n = len(sent)
        copy = pltpu.make_async_remote_copy(
            src_ref=src,
            dst_ref=dst,
            send_sem=send_sems.at[n],
            recv_sem=recv_sems.at[n],
            device_id=peer,
            device_id_type=MESH,
        )
        copy.start()
        sent.append(copy)
        return copy

    def arrive(copies):
        for copy in copies:
            copy.wait_recv()

    def spread(ref, where):
        return [send(ref, ref, where(d)) for d in (1, 3, 2)]

    def lanes(full):
        turned = full.T
        return jnp.where(c == 0, turned[:64], turned[64:])

    def both(mine, other):
        first = jnp.where(c == 0, mine, other)
        second = jnp.where(c == 0, other, mine)
        return jnp.concatenate([first, second], axis=0).T

    def tiles(count, size):
        def wrap(step):
            @pl.loop(0, count // size)
            def _(i):
                step(pl.ds(pl.multiple_of(i * size, size), size))

        return wrap

    def build(ref, base_of, table, first):
        count = ref.shape[0]

        @pl.loop(0, 16)
        def _(k):
            at = pl.multiple_of(lax.rem(k, 8) * 256, 256)
            part = table[pl.ds(first + k // 8, 1), pl.ds(at, 256)]
            for lo in range(0, count, 128):
                target = base_of(lax.broadcasted_iota(I32, (128, 256), 0) + lo)
                hit = jnp.where(jnp.broadcast_to(part, (128, 256)) == target, 1.0, 0.0)
                ref[lo : lo + 128, pl.ds(pl.multiple_of(k * 256, 256), 256)] = hit.astype(BF)

    def wide(src, depth):
        parts = [src[j].reshape(depth, 128) for j in range(4)]
        return jnp.concatenate(parts, axis=1)

    def back_mm(w, start, src, depth, out):
        @tiles(out.shape[1], 128)
        def _(m):
            at = pl.ds(pl.multiple_of(start + m.start, 128), 128)
            r = dot_t(w[:, at], wide(src, depth))
            for j in range(4):
                out[j, m, :] = r[:, j * 128 : (j + 1) * 128].astype(out.dtype)

    def pick(matrix, vec, out):
        @pl.loop(0, 8)
        def _(k):
            r = dot_t(matrix[:, pl.ds(pl.multiple_of(k * 512, 512), 512)], vec[...])
            out[k // 4, lax.rem(k, 4)] = r.astype(BF).reshape(2, 256, 128)

    def hand_on(keep, part, buf, count):
        @tiles(count, 128)
        def _(m):
            buf[m, :] = (keep[m, :] + part[m, :].astype(F32)).astype(BF)

    def tot(part, m):
        return (part[0, m, :].astype(F32) + part[1, m, :].astype(F32)) + part[2, m, :].astype(F32)

    def root_sum(s, k, lo):
        mine = v.f_t[c, s, k, :, lo : lo + 256].astype(F32)
        return mine + v.f_tr[s, k, :, lo : lo + 256].astype(F32)

    def child_base(j):
        return jnp.where(
            j < 384, h * 3072 + row * 384 + j, 6144 - 384 + row * 256 + h * 128 + j
        )

    def root_base(j):
        return (sec * 8 + row) * 384 + j

    def forward():
        need(v.i_cr)
        v.f_x[z] = v.i_cr[...].astype(BF)
        got = spread(v.f_x.at[z], at_z)
        yield
        need(v.cmap)
        build(v.sel, child_base, v.cmap, 2 * p)
        need(v.wci)
        core = []
        order = (0, 1, 3, 2)
        for d in order:
            if d:
                got[order.index(d) - 1].wait_recv()
            ch = (z + 4 - d) % 4
            v.f_ps[ch] = dot(v.wci[pl.ds(sib * 512, 512), :], v.f_x[ch]).astype(BF)
            core.append(send(v.f_ps.at[ch], v.f_pr.at[ch], sibling))
        for ch in range(4):
            v.f_k[ch, :512] = dot(v.wci[pl.ds(c * 512, 512), :], v.f_x[ch])
        yield
        arrive(core)
        got = []
        for d in (1, 3, 2):
            ch = (x + d) % 4
            hand_on(v.f_k.at[ch], v.f_pr.at[ch], v.f_xs.at[d - 1], 512)
            got.append(send(v.f_xs.at[d - 1], v.f_xr.at[d - 1], at_x(d)))
        yield
        arrive(got)

        @tiles(512, 128)
        def _(m):
            own = (v.f_k[x, m, :] + v.f_pr[x, m, :].astype(F32)) + tot(v.f_xr, m)
            v.f_x2[x, c, m, :] = own.astype(BF)
            v.f_u[m, :] = own

        got = spread(v.f_x2.at[x, c], at_x)
        core = [send(v.f_x2.at[x, c], v.f_x2.at[x, c], sibling)]
        up = send(v.f_u, v.f_us, sibling)
        yield
        need(v.wcl)
        for copy, d in zip(got, (1, 3, 2)):
            copy.wait_recv()
            ref = v.f_x2.at[(x + 4 - d) % 4, c]
            core.append(send(ref, ref, sibling))
        yield
        arrive(core)
        got = []
        for d in (1, 3, 2):
            ch = (z + d) % 4
            r = dot(v.wcl[...], v.f_x2[ch].reshape(1024, 128))
            v.f_cs[d - 1] = r.astype(BF)
            got.append(send(v.f_cs.at[d - 1], v.f_cr.at[d - 1], at_z(d)))
        own = dot(v.wcl[...], v.f_x2[z].reshape(1024, 128))
        yield
        arrive(got)
        own = own + (v.f_cr[0].astype(F32) + v.f_cr[1].astype(F32)) + v.f_cr[2].astype(F32)
        v.f_c[h, row] = (-own).astype(BF)
        got = send(v.f_c.at[h, row], v.f_c.at[h, row], pair)
        up.wait_recv()
        v.o_cu[:, pl.ds(pl.multiple_of(c * 512, 128), 512)] = lanes(v.f_u[...])
        v.o_cu[:, pl.ds(pl.multiple_of(sib * 512, 128), 512)] = lanes(v.f_us[...])
        emit(v.o_cu, 0)
        yield
        got.wait_recv()
        got = spread(v.f_c.at[:, row], at_x)
        core = [send(v.f_c.at[:, row], v.f_c.at[:, row], sibling)]
        yield
        need(v.i_pr)
        for copy, d in zip(got, (1, 3, 2)):
            copy.wait_recv()
            ref = v.f_c.at[:, ((x + 4 - d) % 4) * 2 + c]
            core.append(send(ref, ref, sibling))
        yield
        arrive(core)

        @tiles(384, 128)
        def _(m):
            front = dot(v.sel[m, :], v.f_c[...].reshape(4096, 128))
            v.f_px[z, m, :] = (v.i_pr[m, :] + front).astype(BF)

        got = spread(v.f_px.at[z], at_z)
        v.f_fc[...] = dot(v.sel[384:, :], v.f_c[...].reshape(4096, 128))
        yield
        need(v.wpi)
        core = []
        for d in order:
            if d:
                got[order.index(d) - 1].wait_recv()
            ch = (z + 4 - d) % 4
            for half in range(2):
                w = v.wpi[pl.ds(half * 768 + sib * 384, 384), :]
                v.f_qs[ch, half * 384 : (half + 1) * 384] = dot(w, v.f_px[ch]).astype(BF)
            core.append(send(v.f_qs.at[ch], v.f_qr.at[ch], sibling))
        for ch in range(4):
            for half in range(2):
                w = v.wpi[pl.ds(half * 768 + c * 384, 384), :]
                v.f_k[ch, half * 384 : (half + 1) * 384] = dot(w, v.f_px[ch])
        yield
        arrive(core)
        got = []
        for d in (1, 3, 2):
            ch = (x + d) % 4
            hand_on(v.f_k.at[ch], v.f_qr.at[ch], v.f_qxs.at[d - 1], 768)
            got.append(send(v.f_qxs.at[d - 1], v.f_qxr.at[d - 1], at_x(d)))
        yield
        arrive(got)

        @tiles(768, 128)
        def _(m):
            own = v.f_k[x, m, :] + v.f_qr[x, m, :].astype(F32)
            v.f_q[m, :] = own + tot(v.f_qxr, m)

        v.f_qps[...] = v.f_q[pl.ds(oh * 384, 384), :].astype(BF)
        got = send(v.f_qps, v.f_qpr, pair)
        yield
        got.wait_recv()
        own = v.f_q[pl.ds(h * 384, 384), :] + v.f_qpr[...].astype(F32)
        v.f_x3[x, c] = own.astype(BF)
        got = spread(v.f_x3.at[x, c], at_x)
        core = [send(v.f_x3.at[x, c], v.f_x3.at[x, c], sibling)]
        v.f_pu[...] = own
        up = send(v.f_pu, v.f_pus, sibling)
        yield
        need(v.wpl)
        for copy, d in zip(got, (1, 3, 2)):
            copy.wait_recv()
            ref = v.f_x3.at[(x + 4 - d) % 4, c]
            core.append(send(ref, ref, sibling))
        yield
        arrive(core)
        got = []
        for d in (1, 3, 2):
            ch = (z + d) % 4
            r = dot(v.wpl[...], v.f_x3[ch].reshape(768, 128))
            v.f_ds[d - 1] = r.astype(BF)
            got.append(send(v.f_ds.at[d - 1], v.f_dr.at[d - 1], at_z(d)))
        own = dot(v.wpl[...], v.f_x3[z].reshape(768, 128))
        yield
        arrive(got)
        own = own + (v.f_dr[0].astype(F32) + v.f_dr[1].astype(F32)) + v.f_dr[2].astype(F32)
        v.f_up[...] = own.reshape(2, 128, 128)
        v.f_ups[...] = v.f_up[oh].astype(BF)
        got = send(v.f_ups, v.f_upr, pair)
        up.wait_recv()
        v.o_pu[:, pl.ds(pl.multiple_of(c * 384, 128), 384)] = lanes(v.f_pu[...])
        v.o_pu[:, pl.ds(pl.multiple_of(sib * 384, 128), 384)] = lanes(v.f_pus[...])
        emit(v.o_pu, 1)
        yield
        got.wait_recv()
        own = v.f_fc[...] - (v.f_up[h] + v.f_upr[...].astype(F32))
        v.f_r[p, row, h] = own.astype(BF)
        got = spread(v.f_r.at[p, row, h], at_y)
        yield
        arrive(got)
        got = spread(v.f_r.at[:, row], at_x)
        core = [send(v.f_r.at[:, row], v.f_r.at[:, row], sibling)]
        yield
        need(v.i_rr)
        for copy, d in zip(got, (1, 3, 2)):
            copy.wait_recv()
            ref = v.f_r.at[:, ((x + 4 - d) % 4) * 2 + c]
            core.append(send(ref, ref, sibling))
        yield
        arrive(core)

        @tiles(384, 128)
        def _(m):
            front = dot(v.rsel[m, :], v.f_r[...].reshape(4096, 128))
            v.f_rx[z, m, :] = (v.i_rr[m, :] + front).astype(BF)

        got = spread(v.f_rx.at[z], at_z)
        yield
        arrive(got)
        core = []
        for s in range(4):

            @pl.loop(0, 4)
            def _(k):
                start = pl.multiple_of((s * 4 + k) * 192, 192)
                r = dot(v.wr[pl.ds(start, 192), :], wide(v.f_rx, 384))
                v.f_t[0, s, k] = r[:96].astype(BF)
                v.f_t[1, s, k] = r[96:].astype(BF)

            core.append(send(v.f_t.at[sib, s], v.f_tr.at[s], sibling))
        yield
        arrive(core)
        got_a, got_b = [], []
        for d in (1, 3, 2):
            ch = (x + d) % 4

            @pl.loop(0, 4)
            def _(s):
                v.f_as[d - 1, s] = root_sum(s, ch, 0).astype(BF)

            got_a.append(send(v.f_as.at[d - 1], v.f_ar.at[d - 1], at_x(d)))
            cy = (sec + d) % 4

            @pl.loop(0, 4)
            def _(s):
                v.f_bs[d - 1, s] = root_sum(cy, s, 256).astype(BF)

            got_b.append(send(v.f_bs.at[d - 1], v.f_br.at[d - 1], at_y(d)))

        @pl.loop(0, 4)
        def _(s):
            v.f_oa[s] = root_sum(s, x, 0)
            v.f_ob[s] = root_sum(sec, s, 256)

        yield
        for got, total, part in ((got_a, v.f_oa, v.f_ar), (got_b, v.f_ob, v.f_br)):
            arrive(got)

            @pl.loop(0, 4)
            def _(s):
                total[s] = total[s] + (
                    (part[0, s].astype(F32) + part[1, s].astype(F32))
                    + part[2, s].astype(F32)
                )

        got = []
        for d in (1, 3, 2):
            v.f_a2s[d - 1] = v.f_oa[(sec + d) % 4].astype(BF)
            got.append(send(v.f_a2s.at[d - 1], v.f_a2r.at[d - 1], at_y(d)))
            v.f_b2s[d - 1] = v.f_ob[(x + d) % 4].astype(BF)
            got.append(send(v.f_b2s.at[d - 1], v.f_b2r.at[d - 1], at_x(d)))
        yield
        arrive(got)
        for total, me, part, lo in ((v.f_oa, sec, v.f_a2r, 0), (v.f_ob, x, v.f_b2r, 256)):
            v.o_ru[:, lo : lo + 256] = total[me] + (
                (part[0].astype(F32) + part[1].astype(F32)) + part[2].astype(F32)
            )
        emit(v.o_ru, 2)

    def backward():
        need(v.i_rb)
        v.b_y[sec, x, c] = v.i_rb[...].astype(BF)
        ref_a = v.b_y.at[sec, x, c, :, 0:256]
        ref_b = v.b_y.at[sec, x, c, :, 256:512]
        got_a = spread(ref_a, at_x)
        got_b = spread(ref_b, at_y)
        need(v.i_cb, v.i_pb)
        cbs = send(v.i_cb, v.b_cbs, sibling)
        pbs = send(v.i_pb, v.b_pbs, sibling)
        yield
        need(v.pmap)
        build(v.rsel, root_base, v.pmap, 0)
        arrive(got_a)
        got = spread(v.b_y.at[sec, :, c, :, 0:256], at_y)
        arrive(got_b)
        got += spread(v.b_y.at[:, x, c, :, 256:512], at_x)
        yield
        arrive(got)
        core = [send(v.b_y.at[s, :, c], v.b_y.at[s, :, c], sibling) for s in range(4)]
        need(v.wr)
        yield
        for s in range(4):
            core[s].wait_recv()

            @tiles(384, 128)
            def _(m):
                r = dot_t(v.wr[s * 768 : (s + 1) * 768, m], v.b_y[s].reshape(768, 512))
                for j in range(4):
                    part = r[:, j * 128 : (j + 1) * 128]
                    v.b_r[j, m, :] = part if s == 0 else v.b_r[j, m, :] + part

        got = []
        for d in (1, 3, 2):
            v.b_rs[d - 1] = v.b_r[(z + d) % 4].astype(BF)
            got.append(send(v.b_rs.at[d - 1], v.b_rr.at[d - 1], at_z(d)))
        yield
        arrive(got)

        @tiles(384, 128)
        def _(m):
            own = v.b_r[z, m, :] + tot(v.b_rr, m)
            v.o_rx[m, :] = own
            v.b_rx[m, :] = own.astype(BF)

        emit(v.o_rx, 5)
        pick(v.rsel, v.b_rx, v.b_t)
        core = send(v.b_t.at[:, :, sib], v.b_tr, sibling)
        yield
        core.wait_recv()
        got = []
        for d in (1, 3, 2):
            ch = (x + d) % 4
            for q in range(2):
                v.b_txs[d - 1, q] = v.b_t[q, ch, c] + v.b_tr[q, ch]
            got.append(send(v.b_txs.at[d - 1], v.b_txr.at[d - 1], at_x(d)))
        yield
        arrive(got)
        for q in range(2):
            own = v.b_t[q, x, c] + v.b_tr[q, x]
            v.b_tp[q] = own + ((v.b_txr[0, q] + v.b_txr[1, q]) + v.b_txr[2, q])
        got = []
        for d in (1, 3, 2):
            got.append(send(v.b_tp.at[((sec + d) % 4) // 2], v.b_tpr.at[d - 1], at_y(d)))
        yield
        arrive(got)
        v.b_pk[z] = v.b_tp[p] + ((v.b_tpr[0] + v.b_tpr[1]) + v.b_tpr[2])
        got = spread(v.b_pk.at[z], at_z)
        yield
        need(v.wpl)
        arrive(got)
        back_mm(v.wpl, sib * 384, v.b_pk, 256, v.b_es)
        core = [send(v.b_es, v.b_er, sibling)]
        back_mm(v.wpl, c * 384, v.b_pk, 256, v.b_k.at[:, :384])
        yield
        arrive(core)
        got = []
        for d in (1, 3, 2):
            ch = (x + d) % 4
            hand_on(v.b_k.at[ch], v.b_er.at[ch], v.b_exs.at[d - 1], 384)
            got.append(send(v.b_exs.at[d - 1], v.b_exr.at[d - 1], at_x(d)))
        yield
        pbs.wait_recv()
        arrive(got)

        @tiles(384, 128)
        def _(m):
            at = pl.ds(pl.multiple_of(c * 384 + m.start, 128), 128)
            own = v.b_k[x, m, :] + v.b_er[x, m, :].astype(F32)
            own = both(v.i_pb[:, at], v.b_pbs[:, at]) - (own + tot(v.b_exr, m))
            v.b_g[x, h, c, m, :] = own.astype(BF)

        got = send(v.b_g.at[x, h, c], v.b_g.at[x, h, c], pair)
        yield
        got.wait_recv()
        got = spread(v.b_g.at[x, :, c], at_x)
        core = [send(v.b_g.at[x, :, c], v.b_g.at[x, :, c], sibling)]
        yield
        need(v.wpi)
        for copy, d in zip(got, (1, 3, 2)):
            copy.wait_recv()
            ref = v.b_g.at[(x + 4 - d) % 4, :, c]
            core.append(send(ref, ref, sibling))
        yield
        arrive(core)
        back_mm(v.wpi, 0, v.b_g, 1536, v.b_r)
        got = []
        for d in (1, 3, 2):
            v.b_hs[d - 1] = v.b_r[(z + d) % 4].astype(BF)
            got.append(send(v.b_hs.at[d - 1], v.b_hr.at[d - 1], at_z(d)))
        yield
        arrive(got)

        @tiles(384, 128)
        def _(m):
            own = v.b_r[z, m, :] + tot(v.b_hr, m)
            v.o_px[m, :] = own
            v.b_fx[m, :] = own.astype(BF)

        emit(v.o_px, 4)
        v.b_fx[384:, :] = v.b_pk[z, pl.ds(h * 128, 128), :]
        pick(v.sel, v.b_fx, v.b_v)
        core = send(v.b_v.at[:, :, sib], v.b_vr, sibling)
        yield
        core.wait_recv()
        got = []
        for d in (1, 3, 2):
            ch = (x + d) % 4
            for q in range(2):
                v.b_vxs[d - 1, q] = v.b_v[q, ch, c] + v.b_vr[q, ch]
            got.append(send(v.b_vxs.at[d - 1], v.b_vxr.at[d - 1], at_x(d)))
        yield
        arrive(got)
        for q in range(2):
            own = v.b_v[q, x, c] + v.b_vr[q, x]
            v.b_vp[q] = own + ((v.b_vxr[0, q] + v.b_vxr[1, q]) + v.b_vxr[2, q])
        got = send(v.b_vp.at[oh], v.b_vpr, pair)
        yield
        got.wait_recv()
        v.b_ck[z] = v.b_vp[h] + v.b_vpr[...]
        got = spread(v.b_ck.at[z], at_z)
        yield
        need(v.wcl)
        arrive(got)
        back_mm(v.wcl, sib * 512, v.b_ck, 256, v.b_ls)
        core = [send(v.b_ls, v.b_lr, sibling)]
        back_mm(v.wcl, c * 512, v.b_ck, 256, v.b_k)
        yield
        arrive(core)
        got = []
        for d in (1, 3, 2):
            ch = (x + d) % 4
            hand_on(v.b_k.at[ch], v.b_lr.at[ch], v.b_lxs.at[d - 1], 512)
            got.append(send(v.b_lxs.at[d - 1], v.b_lxr.at[d - 1], at_x(d)))
        yield
        cbs.wait_recv()
        arrive(got)

        @tiles(512, 128)
        def _(m):
            at = pl.ds(pl.multiple_of(c * 512 + m.start, 128), 128)
            own = v.b_k[x, m, :] + v.b_lr[x, m, :].astype(F32)
            own = both(v.i_cb[:, at], v.b_cbs[:, at]) - (own + tot(v.b_lxr, m))
            v.b_h[x, c, m, :] = own.astype(BF)

        got = spread(v.b_h.at[x, c], at_x)
        core = [send(v.b_h.at[x, c], v.b_h.at[x, c], sibling)]
        yield
        need(v.wci)
        for copy, d in zip(got, (1, 3, 2)):
            copy.wait_recv()
            ref = v.b_h.at[(x + 4 - d) % 4, c]
            core.append(send(ref, ref, sibling))
        yield
        arrive(core)
        back_mm(v.wci, 0, v.b_h, 1024, v.b_k)
        got = []
        for d in (1, 3, 2):
            v.b_ms[d - 1] = v.b_k[(z + d) % 4].astype(BF)
            got.append(send(v.b_ms.at[d - 1], v.b_mr.at[d - 1], at_z(d)))
        yield
        arrive(got)

        @tiles(512, 128)
        def _(m):
            v.o_cx[m, :] = v.b_k[z, m, :] + tot(v.b_mr, m)

        emit(v.o_cx, 3)

    chains = [backward(), forward()]
    while chains:
        for chain in list(chains):
            try:
                next(chain)
            except StopIteration:
                chains.remove(chain)
    for copy in loads.values():
        copy.wait()
    for copy in sent:
        copy.wait_send()
    for copy in stores:
        copy.wait()


def per_device(*args):
    any_space = pl.BlockSpec(memory_space=pl.ANY)
    shapes = (
        (1, 64, 1024),
        (1, 64, 768),
        (1, 96, 512),
        (1, 512, 128),
        (1, 384, 128),
        (384, 128),
    )
    scratch = [pltpu.VMEM(s, t) for part in (INPUTS, OUTPUTS, SCRATCH) for s, t in part.values()]
    scratch += [
        pltpu.SemaphoreType.DMA((N_REMOTE,)),
        pltpu.SemaphoreType.DMA((N_REMOTE,)),
        pltpu.SemaphoreType.DMA((N_LOCAL,)),
    ]
    args = list(args)
    for i in (10, 11):
        args[i] = jnp.swapaxes(args[i], 1, 2)
    outs = pl.pallas_call(
        body,
        out_shape=tuple(jax.ShapeDtypeStruct(s, F32) for s in shapes),
        in_specs=[any_space] * len(INPUTS),
        out_specs=(any_space,) * len(OUTPUTS),
        scratch_shapes=scratch,
        compiler_params=pltpu.CompilerParams(
            collective_id=0, has_side_effects=True, vmem_limit_bytes=63 * 1024 * 1024
        ),
    )(*args)
    return tuple(jnp.swapaxes(o, 1, 2) if i < 2 else o for i, o in enumerate(outs))


def solution(mesh):
    return jax.shard_map(
        per_device,
        mesh=mesh,
        in_specs=(
            P("sec", "col", "row"),
            P("sec", "row", "col"),
            P("sec", "col", "row"),
            P("sec", "row", "col"),
            P("col", ("sec", "row")),
            P(),
            P(),
            P("sec", "row", "col"),
            P("sec", "row", "col"),
            P(("sec", "row"), "col"),
            P("sec", "col", "row"),
            P("sec", "col", "row"),
            P("col", ("sec", "row"), None),
        ),
        out_specs=(
            P("sec", "col", "row"),
            P("sec", "col", "row"),
            P("col", ("sec", "row"), None),
            P("sec", "row", "col"),
            P("sec", "row", "col"),
            P(("sec", "row"), "col"),
        ),
        check_vma=False,
    )
```

```python
import types

import jax
import jax.numpy as jnp
from jax import lax
from jax.experimental import pallas as pl
from jax.experimental.pallas import tpu as pltpu
from jax.sharding import PartitionSpec as P

BF = jnp.bfloat16
F32 = jnp.float32
I32 = jnp.int32
MESH = pl.DeviceIdType.MESH

INPUTS = dict(
    wci=((1024, 512), BF),
    wcl=((256, 1024), BF),
    wpi=((1536, 384), BF),
    wpl=((256, 768), BF),
    wr=((3072, 384), BF),
    cmap=((4, 2048), I32),
    pmap=((2, 2048), I32),
    i_cr=((512, 128), F32),
    i_pr=((384, 128), F32),
    i_rr=((384, 128), F32),
    i_cb=((64, 1024), F32),
    i_pb=((64, 768), F32),
    i_rb=((96, 512), F32),
)
OUTPUTS = dict(
    o_cu=((64, 1024), F32),
    o_pu=((64, 768), F32),
    o_ru=((96, 512), F32),
    o_cx=((512, 128), F32),
    o_px=((384, 128), F32),
    o_rx=((384, 128), F32),
)
SCRATCH = dict(
    sel=((512, 4096), BF),
    rsel=((384, 4096), BF),
    f_x=((4, 512, 128), BF),
    f_ps=((4, 512, 128), BF),
    f_pr=((4, 512, 128), BF),
    f_xs=((3, 512, 128), BF),
    f_xr=((3, 512, 128), BF),
    f_u=((512, 128), F32),
    f_us=((512, 128), F32),
    f_x2=((4, 2, 512, 128), BF),
    f_cs=((3, 256, 128), BF),
    f_cr=((3, 256, 128), BF),
    f_c=((2, 8, 256, 128), BF),
    f_px=((4, 384, 128), BF),
    f_qs=((4, 768, 128), BF),
    f_k=((4, 768, 128), F32),
    f_qr=((4, 768, 128), BF),
    f_qxs=((7, 384, 128), BF),
    f_qxr=((7, 384, 128), BF),
    f_pu=((384, 128), F32),
    f_pus=((384, 128), F32),
    f_x3=((4, 2, 384, 128), BF),
    f_ds=((7, 128, 128), BF),
    f_dr=((7, 128, 128), BF),
    f_uk=((4, 256, 128), F32),
    f_fr=((512, 128), F32),
    f_r=((2, 8, 2, 128, 128), BF),
    f_rx=((4, 384, 128), BF),
    f_t=((2, 4, 4, 96, 512), BF),
    f_tr=((4, 4, 96, 512), BF),
    f_as=((3, 4, 96, 256), BF),
    f_bs=((3, 4, 96, 256), BF),
    f_ar=((3, 4, 96, 256), BF),
    f_br=((3, 4, 96, 256), BF),
    f_oa=((4, 96, 256), F32),
    f_ob=((4, 96, 256), F32),
    f_a2s=((3, 96, 256), BF),
    f_b2s=((3, 96, 256), BF),
    f_a2r=((3, 96, 256), BF),
    f_b2r=((3, 96, 256), BF),
    b_y=((4, 4, 2, 96, 512), BF),
    b_r=((4, 384, 128), F32),
    b_rs=((3, 384, 128), BF),
    b_rr=((3, 384, 128), BF),
    b_rx=((384, 128), BF),
    b_t=((2, 4, 2, 256, 128), BF),
    b_tr=((2, 4, 256, 128), BF),
    b_txs=((3, 2, 256, 128), BF),
    b_txr=((3, 2, 256, 128), BF),
    b_tp=((2, 256, 128), BF),
    b_tpr=((3, 256, 128), BF),
    b_pk=((4, 256, 128), BF),
    b_es=((4, 384, 128), BF),
    b_er=((4, 384, 128), BF),
    b_exs=((3, 384, 128), BF),
    b_exr=((3, 384, 128), BF),
    b_pbs=((64, 768), F32),
    b_g=((4, 2, 2, 384, 128), BF),
    b_hs=((3, 384, 128), BF),
    b_hr=((3, 384, 128), BF),
    b_fx=((512, 128), BF),
    b_v=((2, 4, 2, 256, 128), BF),
    b_vr=((2, 4, 256, 128), BF),
    b_vxs=((7, 256, 128), BF),
    b_vxr=((7, 256, 128), BF),
    b_ck=((4, 256, 128), BF),
    b_ls=((4, 512, 128), BF),
    b_k=((4, 512, 128), F32),
    b_lr=((4, 512, 128), BF),
    b_lxs=((3, 512, 128), BF),
    b_lxr=((3, 512, 128), BF),
    b_cbs=((64, 1024), F32),
    b_h=((4, 2, 512, 128), BF),
    b_ms=((3, 512, 128), BF),
    b_mr=((3, 512, 128), BF),
)
N_REMOTE = 260
N_LOCAL = len(INPUTS) + len(OUTPUTS)


def dot(a, b):
    return jnp.dot(a, b, preferred_element_type=F32)


def dot_t(a, b):
    return lax.dot_general(a, b, (((0,), (0,)), ((), ())), preferred_element_type=F32)


def body(*refs):
    n_in, n_out = len(INPUTS), len(OUTPUTS)
    hbm_in = refs[:n_in]
    hbm_out = refs[n_in : n_in + n_out]
    rest = refs[n_in + n_out :]
    names = [*INPUTS, *OUTPUTS, *SCRATCH]
    v = types.SimpleNamespace(**dict(zip(names, rest)))
    send_sems, recv_sems, local_sems = rest[len(names) :]

    sec = lax.axis_index("sec")
    row = lax.axis_index("row")
    z = lax.axis_index("col")
    x = row // 2
    c = row % 2
    sib = 1 - c
    h = sec % 2
    p = sec // 2
    oh = 1 - h

    def at_x(d):
        return {"row": ((x + d) % 4) * 2 + c}

    def at_y(d):
        return {"sec": (sec + d) % 4}

    def at_z(d):
        return {"col": (z + d) % 4}

    def at_xy(dx, dy):
        return {"row": ((x + dx) % 4) * 2 + c, "sec": (sec + dy) % 4}

    def at_px(d, q):
        return {"row": ((x + d) % 4) * 2 + c, "sec": p * 2 + (oh if q else h)}

    def at_pz(d, q):
        return {"col": (z + d) % 4, "sec": p * 2 + (oh if q else h)}

    sibling = {"row": x * 2 + sib}
    near = (0, 1, 3, 2)
    eight = [(0, 1)] + [(d, q) for d in (1, 3, 2) for q in (0, 1)]

    loads = {}
    for i, (ref, src) in enumerate(zip(rest, hbm_in)):
        if len(src.shape) > len(ref.shape):
            src = src.at[0]
        loads[id(ref)] = pltpu.make_async_copy(src, ref, local_sems.at[i])
    first = (v.i_rb, v.i_cr, v.i_cb, v.i_pb, v.wci, v.wr, v.cmap, v.pmap)
    for ref in first + (v.wcl, v.i_pr, v.wpi, v.wpl, v.i_rr):
        loads[id(ref)].start()

    def need(*wanted):
        for ref in wanted:
            copy = loads.pop(id(ref), None)
            if copy is not None:
                copy.wait()

    stores = []

    def emit(ref, i):
        dst = hbm_out[i]
        if len(dst.shape) > 2:
            dst = dst.at[0]
        copy = pltpu.make_async_copy(ref, dst, local_sems.at[n_in + i])
        copy.start()
        stores.append(copy)

    barrier = pltpu.get_barrier_semaphore()
    peers = [sibling] + [at_z(d) for d in (1, 2, 3)] + [at_pz(d, 1) for d in (1, 2, 3)]
    peers += [at_xy(dx, dy) for dx in range(4) for dy in range(4) if dx or dy]
    for peer in peers:
        pl.semaphore_signal(barrier, inc=1, device_id=peer, device_id_type=MESH)
    pl.semaphore_wait(barrier, len(peers))

    sent = []

    def send(src, dst, peer):
        n = len(sent)
        copy = pltpu.make_async_remote_copy(
            src_ref=src,
            dst_ref=dst,
            send_sem=send_sems.at[n],
            recv_sem=recv_sems.at[n],
            device_id=peer,
            device_id_type=MESH,
        )
        copy.start()
        sent.append(copy)
        return copy

    def arrive(copies):
        for copy in copies:
            copy.wait_recv()

    def spread(ref, where):
        return [send(ref, ref, where(d)) for d in (1, 3, 2)]

    def lanes(full):
        turned = full.T
        return jnp.where(c == 0, turned[:64], turned[64:])

    def both(mine, other):
        first = jnp.where(c == 0, mine, other)
        second = jnp.where(c == 0, other, mine)
        return jnp.concatenate([first, second], axis=0).T

    def tiles(count, size):
        def wrap(step):
            @pl.loop(0, count // size)
            def _(i):
                step(pl.ds(pl.multiple_of(i * size, size), size))

        return wrap

    def slot(d, q):
        return 3 + d if q else d - 1

    def tot7(part, m):
        return tot(part, m) + (
            (part[3, m, :].astype(F32) + part[4, m, :].astype(F32))
            + (part[5, m, :].astype(F32) + part[6, m, :].astype(F32))
        )

    def hand_over(ref, got):
        core = []
        for d in near:
            arrive(got[d])
            part = ref((x + 4 - d) % 4)
            core.append(send(part, part, sibling))
        return core

    def select(core, matrix, src, out):
        rows = matrix.shape[0]
        for i, d in enumerate(near):
            core[i].wait_recv()
            ch = (x + 4 - d) % 4
            for q in range(2):
                at = pl.ds(pl.multiple_of(q * 2048 + ch * 512, 512), 512)
                r = dot(matrix[:, at], src[q, pl.ds(2 * ch, 2)].reshape(512, 128))
                if i == 0 and q == 0:
                    out[:rows, :] = r
                else:
                    out[:rows, :] = out[:rows, :] + r

    def build(ref, base_of, table, first):
        count = ref.shape[0]

        @pl.loop(0, 16)
        def _(k):
            at = pl.multiple_of(lax.rem(k, 8) * 256, 256)
            part = table[pl.ds(first + k // 8, 1), pl.ds(at, 256)]
            for lo in range(0, count, 128):
                target = base_of(lax.broadcasted_iota(I32, (128, 256), 0) + lo)
                hit = jnp.where(jnp.broadcast_to(part, (128, 256)) == target, 1.0, 0.0)
                ref[lo : lo + 128, pl.ds(pl.multiple_of(k * 256, 256), 256)] = hit.astype(BF)

    def wide(src, depth):
        parts = [src[j].reshape(depth, 128) for j in range(4)]
        return jnp.concatenate(parts, axis=1)

    def back_mm(w, start, src, depth, out):
        @tiles(out.shape[1], 128)
        def _(m):
            at = pl.ds(pl.multiple_of(start + m.start, 128), 128)
            r = dot_t(w[:, at], wide(src, depth))
            for j in range(4):
                out[j, m, :] = r[:, j * 128 : (j + 1) * 128].astype(out.dtype)

    def pick(matrix, vec, out, part):
        core = []
        for q in range(2):

            @pl.loop(0, 4)
            def _(k):
                at = pl.multiple_of(q * 2048 + k * 512, 512)
                r = dot_t(matrix[:, pl.ds(at, 512)], vec[...])
                out[q, k] = r.astype(BF).reshape(2, 256, 128)

            core.append(send(out.at[q, :, sib], part.at[q], sibling))
        return core

    def hand_on(keep, part, buf, count):
        @tiles(count, 128)
        def _(m):
            buf[m, :] = (keep[m, :] + part[m, :].astype(F32)).astype(BF)

    def tot(part, m):
        return (part[0, m, :].astype(F32) + part[1, m, :].astype(F32)) + part[2, m, :].astype(F32)

    def root_sum(s, k, lo):
        mine = v.f_t[c, s, k, :, lo : lo + 256].astype(F32)
        return mine + v.f_tr[s, k, :, lo : lo + 256].astype(F32)

    def child_base(j):
        return jnp.where(
            j < 384, h * 3072 + row * 384 + j, 6144 - 384 + row * 256 + h * 128 + j
        )

    def root_base(j):
        return (sec * 8 + row) * 384 + j

    def forward():
        need(v.i_cr)
        v.f_x[z] = v.i_cr[...].astype(BF)
        got = spread(v.f_x.at[z], at_z)
        yield
        need(v.cmap)
        build(v.sel, child_base, v.cmap, 2 * p)
        need(v.wci)
        core = []
        order = (0, 1, 3, 2)
        for d in order:
            if d:
                got[order.index(d) - 1].wait_recv()
            ch = (z + 4 - d) % 4
            v.f_ps[ch] = dot(v.wci[pl.ds(sib * 512, 512), :], v.f_x[ch]).astype(BF)
            core.append(send(v.f_ps.at[ch], v.f_pr.at[ch], sibling))
        for ch in range(4):
            v.f_k[ch, :512] = dot(v.wci[pl.ds(c * 512, 512), :], v.f_x[ch])
        yield
        arrive(core)
        got = []
        for d in (1, 3, 2):
            ch = (x + d) % 4
            hand_on(v.f_k.at[ch], v.f_pr.at[ch], v.f_xs.at[d - 1], 512)
            got.append(send(v.f_xs.at[d - 1], v.f_xr.at[d - 1], at_x(d)))
        yield
        arrive(got)

        @tiles(512, 128)
        def _(m):
            own = (v.f_k[x, m, :] + v.f_pr[x, m, :].astype(F32)) + tot(v.f_xr, m)
            v.f_x2[x, c, m, :] = own.astype(BF)
            v.f_u[m, :] = own

        got = spread(v.f_x2.at[x, c], at_x)
        core = [send(v.f_x2.at[x, c], v.f_x2.at[x, c], sibling)]
        up = send(v.f_u, v.f_us, sibling)
        yield
        need(v.wcl)
        for copy, d in zip(got, (1, 3, 2)):
            copy.wait_recv()
            ref = v.f_x2.at[(x + 4 - d) % 4, c]
            core.append(send(ref, ref, sibling))
        yield
        arrive(core)
        got = []
        for d in (1, 3, 2):
            ch = (z + d) % 4
            r = dot(v.wcl[...], v.f_x2[ch].reshape(1024, 128))
            v.f_cs[d - 1] = r.astype(BF)
            got.append(send(v.f_cs.at[d - 1], v.f_cr.at[d - 1], at_z(d)))
        own = dot(v.wcl[...], v.f_x2[z].reshape(1024, 128))
        yield
        arrive(got)
        own = own + (v.f_cr[0].astype(F32) + v.f_cr[1].astype(F32)) + v.f_cr[2].astype(F32)
        v.f_c[h, row] = (-own).astype(BF)
        got = {d: [] for d in near}
        for d, q in eight:
            got[d].append(send(v.f_c.at[h, row], v.f_c.at[h, row], at_px(d, q)))
        up.wait_recv()
        v.o_cu[:, pl.ds(pl.multiple_of(c * 512, 128), 512)] = lanes(v.f_u[...])
        v.o_cu[:, pl.ds(pl.multiple_of(sib * 512, 128), 512)] = lanes(v.f_us[...])
        emit(v.o_cu, 0)
        yield
        need(v.i_pr)
        core = hand_over(lambda k: v.f_c.at[:, 2 * k + c], got)
        yield
        select(core, v.sel, v.f_c, v.f_fr)

        @tiles(384, 128)
        def _(m):
            v.f_px[z, m, :] = (v.i_pr[m, :] + v.f_fr[m, :]).astype(BF)

        got = spread(v.f_px.at[z], at_z)
        yield
        need(v.wpi)
        core = []
        for d in order:
            if d:
                got[order.index(d) - 1].wait_recv()
            ch = (z + 4 - d) % 4
            for half in range(2):
                w = v.wpi[pl.ds(half * 768 + sib * 384, 384), :]
                v.f_qs[ch, half * 384 : (half + 1) * 384] = dot(w, v.f_px[ch]).astype(BF)
            core.append(send(v.f_qs.at[ch], v.f_qr.at[ch], sibling))
        for ch in range(4):
            for half in range(2):
                w = v.wpi[pl.ds(half * 768 + c * 384, 384), :]
                v.f_k[ch, half * 384 : (half + 1) * 384] = dot(w, v.f_px[ch])
        yield
        arrive(core)
        got = []
        for d, q in eight[1:] + eight[:1]:
            ch = (x + d) % 4
            at = pl.ds(pl.multiple_of((oh if q else h) * 384, 128), 384)
            buf = v.f_qxs.at[slot(d, q)]
            hand_on(v.f_k.at[ch, at], v.f_qr.at[ch, at], buf, 384)
            got.append(send(buf, v.f_qxr.at[slot(d, q)], at_px(d, q)))
        yield
        arrive(got)

        @tiles(384, 128)
        def _(m):
            at = pl.ds(pl.multiple_of(h * 384 + m.start, 128), 128)
            own = v.f_k[x, at, :] + v.f_qr[x, at, :].astype(F32) + tot7(v.f_qxr, m)
            v.f_pu[m, :] = own
            v.f_x3[x, c, m, :] = own.astype(BF)

        got = spread(v.f_x3.at[x, c], at_x)
        core = [send(v.f_x3.at[x, c], v.f_x3.at[x, c], sibling)]
        up = send(v.f_pu, v.f_pus, sibling)
        yield
        need(v.wpl)
        for copy, d in zip(got, (1, 3, 2)):
            copy.wait_recv()
            ref = v.f_x3.at[(x + 4 - d) % 4, c]
            core.append(send(ref, ref, sibling))
        yield
        arrive(core)
        got = []
        for d in (1, 3, 2, 0):
            ch = (z + d) % 4
            v.f_uk[ch] = dot(v.wpl[...], v.f_x3[ch].reshape(768, 128))
            for q in (0, 1):
                if d or q:
                    at = pl.ds(pl.multiple_of((oh if q else h) * 128, 128), 128)
                    v.f_ds[slot(d, q)] = v.f_uk[ch, at, :].astype(BF)
                    got.append(send(v.f_ds.at[slot(d, q)], v.f_dr.at[slot(d, q)], at_pz(d, q)))
        up.wait_recv()
        v.o_pu[:, pl.ds(pl.multiple_of(c * 384, 128), 384)] = lanes(v.f_pu[...])
        v.o_pu[:, pl.ds(pl.multiple_of(sib * 384, 128), 384)] = lanes(v.f_pus[...])
        emit(v.o_pu, 1)
        yield
        arrive(got)
        own = v.f_uk[z, pl.ds(h * 128, 128), :] + tot7(v.f_dr, slice(None))
        v.f_r[p, row, h] = (v.f_fr[384:, :] - own).astype(BF)
        got = {d: [] for d in near}
        for dx in near:
            for dy in near:
                if dx or dy:
                    ref = v.f_r.at[p, row, h]
                    got[dx].append(send(ref, ref, at_xy(dx, dy)))
        yield
        need(v.i_rr)
        core = hand_over(lambda k: v.f_r.at[:, 2 * k + c], got)
        yield
        select(core, v.rsel, v.f_r, v.f_fr)

        @tiles(384, 128)
        def _(m):
            v.f_rx[z, m, :] = (v.i_rr[m, :] + v.f_fr[m, :]).astype(BF)

        got = spread(v.f_rx.at[z], at_z)
        yield
        arrive(got)
        core = []
        for dy in (1, 3, 2, 0):
            s = (sec + dy) % 4

            @pl.loop(0, 2)
            def _(k):
                start = pl.multiple_of(s * 768 + k * 384, 384)
                r = dot(v.wr[pl.ds(start, 384), :], wide(v.f_rx, 384))
                for j in range(2):
                    for cc in range(2):
                        at = (2 * j + cc) * 96
                        v.f_t[cc, s, 2 * k + j] = r[at : at + 96].astype(BF)

            core.append(send(v.f_t.at[sib, s], v.f_tr.at[s], sibling))
        yield
        got_a, got_b = [], []
        for i, dy in enumerate((1, 3, 2, 0)):
            s = (sec + dy) % 4
            core[i].wait_recv()
            if dy:

                @pl.loop(0, 4)
                def _(k):
                    v.f_bs[dy - 1, k] = root_sum(s, k, 256).astype(BF)

                got_b.append(send(v.f_bs.at[dy - 1], v.f_br.at[dy - 1], at_y(dy)))
            else:

                @pl.loop(0, 4)
                def _(k):
                    v.f_ob[k] = root_sum(s, k, 256)

            part = []
            for d in (1, 3, 2):
                v.f_as[d - 1, s] = root_sum(s, (x + d) % 4, 0).astype(BF)
                part.append(send(v.f_as.at[d - 1, s], v.f_ar.at[d - 1, s], at_x(d)))
            got_a.append(part)
            v.f_oa[s] = root_sum(s, x, 0)
        yield

        def gathered(total, part, k):
            return total[k] + (
                (part[0, k].astype(F32) + part[1, k].astype(F32)) + part[2, k].astype(F32)
            )

        got = []
        for i, dy in enumerate((1, 3, 2, 0)):
            s = (sec + dy) % 4
            arrive(got_a[i])
            if dy:
                v.f_a2s[dy - 1] = gathered(v.f_oa, v.f_ar, s).astype(BF)
                got.append(send(v.f_a2s.at[dy - 1], v.f_a2r.at[dy - 1], at_y(dy)))
            else:
                v.f_oa[s] = gathered(v.f_oa, v.f_ar, s)
        arrive(got_b)
        for d in (1, 3, 2):
            v.f_b2s[d - 1] = gathered(v.f_ob, v.f_br, (x + d) % 4).astype(BF)
            got.append(send(v.f_b2s.at[d - 1], v.f_b2r.at[d - 1], at_x(d)))
        v.f_ob[x] = gathered(v.f_ob, v.f_br, x)
        yield
        arrive(got)
        for total, me, part, lo in ((v.f_oa, sec, v.f_a2r, 0), (v.f_ob, x, v.f_b2r, 256)):
            v.o_ru[:, lo : lo + 256] = total[me] + (
                (part[0].astype(F32) + part[1].astype(F32)) + part[2].astype(F32)
            )
        emit(v.o_ru, 2)

    def backward():
        need(v.i_rb)
        v.b_y[sec, x, c] = v.i_rb[...].astype(BF)
        got_x = spread(v.b_y.at[sec, x, c], at_x)
        got_y = spread(v.b_y.at[sec, x, c], at_y)
        need(v.i_cb, v.i_pb)
        cbs = send(v.i_cb, v.b_cbs, sibling)
        pbs = send(v.i_pb, v.b_pbs, sibling)
        yield
        need(v.pmap)
        build(v.rsel, root_base, v.pmap, 0)
        got_a, got_b = [], []
        for i, d in enumerate((1, 3, 2)):
            got_x[i].wait_recv()
            got_a.append(spread(v.b_y.at[sec, (x + 4 - d) % 4, c, :, 0:256], at_y))
            got_y[i].wait_recv()
            got_b.append(spread(v.b_y.at[(sec + 4 - d) % 4, x, c, :, 256:512], at_x))
        core = [send(v.b_y.at[sec, :, c], v.b_y.at[sec, :, c], sibling)]
        yield
        for i, d in enumerate((1, 3, 2)):
            arrive([part[i] for part in got_a])
            arrive(got_b[i])
            ref = v.b_y.at[(sec + 4 - d) % 4, :, c]
            core.append(send(ref, ref, sibling))
        need(v.wr)
        yield
        for i, d in enumerate(near):
            core[i].wait_recv()
            s = (sec + 4 - d) % 4

            @tiles(384, 128)
            def _(m):
                w = v.wr[pl.ds(pl.multiple_of(s * 768, 768), 768), m]
                r = dot_t(w, v.b_y[s].reshape(768, 512))
                for j in range(4):
                    part = r[:, j * 128 : (j + 1) * 128]
                    v.b_r[j, m, :] = part if i == 0 else v.b_r[j, m, :] + part

        got = []
        for d in (1, 3, 2):
            v.b_rs[d - 1] = v.b_r[(z + d) % 4].astype(BF)
            got.append(send(v.b_rs.at[d - 1], v.b_rr.at[d - 1], at_z(d)))
        yield
        arrive(got)

        @tiles(384, 128)
        def _(m):
            own = v.b_r[z, m, :] + tot(v.b_rr, m)
            v.o_rx[m, :] = own
            v.b_rx[m, :] = own.astype(BF)

        emit(v.o_rx, 5)
        core = pick(v.rsel, v.b_rx, v.b_t, v.b_tr)
        yield
        arrive(core)
        got = []
        for d in (1, 3, 2):
            ch = (x + d) % 4
            for q in range(2):
                v.b_txs[d - 1, q] = v.b_t[q, ch, c] + v.b_tr[q, ch]
            got.append(send(v.b_txs.at[d - 1], v.b_txr.at[d - 1], at_x(d)))
        yield
        arrive(got)
        for q in range(2):
            own = v.b_t[q, x, c] + v.b_tr[q, x]
            v.b_tp[q] = own + ((v.b_txr[0, q] + v.b_txr[1, q]) + v.b_txr[2, q])
        got = []
        for d in (1, 3, 2):
            got.append(send(v.b_tp.at[((sec + d) % 4) // 2], v.b_tpr.at[d - 1], at_y(d)))
        yield
        arrive(got)
        v.b_pk[z] = v.b_tp[p] + ((v.b_tpr[0] + v.b_tpr[1]) + v.b_tpr[2])
        got = spread(v.b_pk.at[z], at_z)
        yield
        need(v.wpl)
        arrive(got)
        back_mm(v.wpl, sib * 384, v.b_pk, 256, v.b_es)
        core = [send(v.b_es, v.b_er, sibling)]
        back_mm(v.wpl, c * 384, v.b_pk, 256, v.b_k.at[:, :384])
        yield
        arrive(core)
        got = []
        for d in (1, 3, 2):
            ch = (x + d) % 4
            hand_on(v.b_k.at[ch], v.b_er.at[ch], v.b_exs.at[d - 1], 384)
            got.append(send(v.b_exs.at[d - 1], v.b_exr.at[d - 1], at_x(d)))
        yield
        pbs.wait_recv()
        arrive(got)

        @tiles(384, 128)
        def _(m):
            at = pl.ds(pl.multiple_of(c * 384 + m.start, 128), 128)
            own = v.b_k[x, m, :] + v.b_er[x, m, :].astype(F32)
            own = both(v.i_pb[:, at], v.b_pbs[:, at]) - (own + tot(v.b_exr, m))
            v.b_g[x, h, c, m, :] = own.astype(BF)

        got = {d: [] for d in near}
        for d, q in eight:
            got[d].append(send(v.b_g.at[x, h, c], v.b_g.at[x, h, c], at_px(d, q)))
        yield
        need(v.wpi)
        core = hand_over(lambda k: v.b_g.at[k, :, c], got)
        yield
        arrive(core)
        back_mm(v.wpi, 0, v.b_g, 1536, v.b_r)
        got = []
        for d in (1, 3, 2):
            v.b_hs[d - 1] = v.b_r[(z + d) % 4].astype(BF)
            got.append(send(v.b_hs.at[d - 1], v.b_hr.at[d - 1], at_z(d)))
        yield
        arrive(got)

        @tiles(384, 128)
        def _(m):
            own = v.b_r[z, m, :] + tot(v.b_hr, m)
            v.o_px[m, :] = own
            v.b_fx[m, :] = own.astype(BF)

        emit(v.o_px, 4)
        v.b_fx[384:, :] = v.b_pk[z, pl.ds(h * 128, 128), :]
        core = pick(v.sel, v.b_fx, v.b_v, v.b_vr)
        yield
        arrive(core)
        got = []
        for d, q in eight[1:] + eight[:1]:
            ch = (x + d) % 4
            a = oh if q else h
            v.b_vxs[slot(d, q)] = v.b_v[a, ch, c] + v.b_vr[a, ch]
            got.append(send(v.b_vxs.at[slot(d, q)], v.b_vxr.at[slot(d, q)], at_px(d, q)))
        yield
        arrive(got)
        own = v.b_v[h, x, c] + v.b_vr[h, x] + (v.b_vxr[0] + v.b_vxr[1] + v.b_vxr[2])
        own = own + ((v.b_vxr[3] + v.b_vxr[4]) + (v.b_vxr[5] + v.b_vxr[6]))
        v.b_ck[z] = own
        got = spread(v.b_ck.at[z], at_z)
        yield
        need(v.wcl)
        arrive(got)
        back_mm(v.wcl, sib * 512, v.b_ck, 256, v.b_ls)
        core = [send(v.b_ls, v.b_lr, sibling)]
        back_mm(v.wcl, c * 512, v.b_ck, 256, v.b_k)
        yield
        arrive(core)
        got = []
        for d in (1, 3, 2):
            ch = (x + d) % 4
            hand_on(v.b_k.at[ch], v.b_lr.at[ch], v.b_lxs.at[d - 1], 512)
            got.append(send(v.b_lxs.at[d - 1], v.b_lxr.at[d - 1], at_x(d)))
        yield
        cbs.wait_recv()
        arrive(got)

        @tiles(512, 128)
        def _(m):
            at = pl.ds(pl.multiple_of(c * 512 + m.start, 128), 128)
            own = v.b_k[x, m, :] + v.b_lr[x, m, :].astype(F32)
            own = both(v.i_cb[:, at], v.b_cbs[:, at]) - (own + tot(v.b_lxr, m))
            v.b_h[x, c, m, :] = own.astype(BF)

        got = spread(v.b_h.at[x, c], at_x)
        core = [send(v.b_h.at[x, c], v.b_h.at[x, c], sibling)]
        yield
        need(v.wci)
        for copy, d in zip(got, (1, 3, 2)):
            copy.wait_recv()
            ref = v.b_h.at[(x + 4 - d) % 4, c]
            core.append(send(ref, ref, sibling))
        yield
        arrive(core)
        back_mm(v.wci, 0, v.b_h, 1024, v.b_k)
        got = []
        for d in (1, 3, 2):
            v.b_ms[d - 1] = v.b_k[(z + d) % 4].astype(BF)
            got.append(send(v.b_ms.at[d - 1], v.b_mr.at[d - 1], at_z(d)))
        yield
        arrive(got)

        @tiles(512, 128)
        def _(m):
            v.o_cx[m, :] = v.b_k[z, m, :] + tot(v.b_mr, m)

        emit(v.o_cx, 3)

    chains = [backward(), forward()]
    while chains:
        for chain in list(chains):
            try:
                next(chain)
            except StopIteration:
                chains.remove(chain)
    for copy in loads.values():
        copy.wait()
    for copy in sent:
        copy.wait_send()
    for copy in stores:
        copy.wait()


def write_out(*refs):
    n = len(OUTPUTS)
    copies = [
        pltpu.make_async_copy(refs[i], refs[n + i], refs[2 * n].at[i]) for i in range(n)
    ]
    for copy in copies:
        copy.start()
    for copy in copies:
        copy.wait()


def per_device(*args):
    any_space = pl.BlockSpec(memory_space=pl.ANY)
    shapes = (
        (1, 64, 1024),
        (1, 64, 768),
        (1, 96, 512),
        (1, 512, 128),
        (1, 384, 128),
        (384, 128),
    )
    scratch = [pltpu.VMEM(s, t) for part in (INPUTS, OUTPUTS, SCRATCH) for s, t in part.values()]
    scratch += [
        pltpu.SemaphoreType.DMA((N_REMOTE,)),
        pltpu.SemaphoreType.DMA((N_REMOTE,)),
        pltpu.SemaphoreType.DMA((N_LOCAL,)),
    ]
    args = list(args)
    for i in (10, 11):
        args[i] = jnp.swapaxes(args[i], 1, 2)
    outs = pl.pallas_call(
        body,
        out_shape=tuple(jax.ShapeDtypeStruct(s, F32) for s in shapes),
        in_specs=[any_space] * len(INPUTS),
        out_specs=(any_space,) * len(OUTPUTS),
        scratch_shapes=scratch,
        compiler_params=pltpu.CompilerParams(
            collective_id=0, has_side_effects=True, vmem_limit_bytes=63 * 1024 * 1024
        ),
    )(*args)
    outs = pl.pallas_call(
        write_out,
        out_shape=tuple(jax.ShapeDtypeStruct(s, F32) for s in shapes),
        in_specs=[any_space] * len(OUTPUTS),
        out_specs=(any_space,) * len(OUTPUTS),
        scratch_shapes=[pltpu.SemaphoreType.DMA((len(OUTPUTS),))],
    )(*outs)
    return tuple(jnp.swapaxes(o, 1, 2) if i < 2 else o for i, o in enumerate(outs))


def solution(mesh):
    return jax.shard_map(
        per_device,
        mesh=mesh,
        in_specs=(
            P("sec", "col", "row"),
            P("sec", "row", "col"),
            P("sec", "col", "row"),
            P("sec", "row", "col"),
            P("col", ("sec", "row")),
            P(),
            P(),
            P("sec", "row", "col"),
            P("sec", "row", "col"),
            P(("sec", "row"), "col"),
            P("sec", "col", "row"),
            P("sec", "col", "row"),
            P("col", ("sec", "row"), None),
        ),
        out_specs=(
            P("sec", "col", "row"),
            P("sec", "col", "row"),
            P("col", ("sec", "row"), None),
            P("sec", "row", "col"),
            P("sec", "row", "col"),
            P(("sec", "row"), "col"),
        ),
        check_vma=False,
    )
```

```python
import types

import jax
import jax.numpy as jnp
from jax import lax
from jax.experimental import pallas as pl
from jax.experimental.pallas import tpu as pltpu
from jax.sharding import PartitionSpec as P

BF = jnp.bfloat16
F32 = jnp.float32
I32 = jnp.int32
MESH = pl.DeviceIdType.MESH

INPUTS = dict(
    wci=((1024, 512), BF),
    wcl=((256, 1024), BF),
    wpi=((1536, 384), BF),
    wpl=((256, 768), BF),
    wr=((3072, 384), BF),
    cmap=((4, 2048), I32),
    pmap=((2, 2048), I32),
    i_cr=((512, 128), F32),
    i_pr=((384, 128), F32),
    i_rr=((384, 128), F32),
    i_cb=((64, 1024), F32),
    i_pb=((64, 768), F32),
    i_rb=((96, 512), F32),
)
OUTPUTS = dict(
    o_cu=((64, 1024), F32),
    o_pu=((64, 768), F32),
    o_ru=((96, 512), F32),
    o_cx=((512, 128), F32),
    o_px=((384, 128), F32),
    o_rx=((384, 128), F32),
)
SCRATCH = dict(
    sel=((512, 4096), BF),
    rsel=((384, 4096), BF),
    f_x=((4, 512, 128), BF),
    f_ps=((4, 512, 128), BF),
    f_pr=((4, 512, 128), BF),
    f_xs=((3, 512, 128), BF),
    f_xr=((3, 512, 128), BF),
    f_u=((512, 128), F32),
    f_us=((512, 128), F32),
    f_x2=((4, 2, 512, 128), BF),
    f_cs=((3, 256, 128), BF),
    f_cr=((3, 256, 128), BF),
    f_c=((2, 8, 256, 128), BF),
    f_px=((4, 384, 128), BF),
    f_qs=((4, 768, 128), BF),
    f_k=((4, 768, 128), F32),
    f_qr=((4, 768, 128), BF),
    f_qxs=((7, 384, 128), BF),
    f_qxr=((7, 384, 128), BF),
    f_pu=((384, 128), F32),
    f_pus=((384, 128), F32),
    f_x3=((4, 2, 384, 128), BF),
    f_ds=((7, 128, 128), BF),
    f_dr=((7, 128, 128), BF),
    f_uk=((4, 256, 128), F32),
    f_fr=((512, 128), F32),
    f_r=((2, 8, 2, 128, 128), BF),
    f_rx=((4, 384, 128), BF),
    f_t=((2, 4, 4, 96, 512), BF),
    f_tr=((4, 4, 96, 512), BF),
    f_as=((3, 4, 96, 256), BF),
    f_bs=((3, 4, 96, 256), BF),
    f_ar=((3, 4, 96, 256), BF),
    f_br=((3, 4, 96, 256), BF),
    f_oa=((4, 96, 256), F32),
    f_ob=((4, 96, 256), F32),
    f_a2s=((3, 96, 256), BF),
    f_b2s=((3, 96, 256), BF),
    f_a2r=((3, 96, 256), BF),
    f_b2r=((3, 96, 256), BF),
    b_y=((4, 4, 2, 96, 512), BF),
    b_r=((4, 384, 128), F32),
    b_rs=((3, 384, 128), BF),
    b_rr=((3, 384, 128), BF),
    b_rx=((384, 128), BF),
    b_t=((2, 4, 2, 256, 128), BF),
    b_tr=((2, 4, 256, 128), BF),
    b_txs=((3, 2, 256, 128), BF),
    b_txr=((3, 2, 256, 128), BF),
    b_tp=((2, 256, 128), BF),
    b_tpr=((3, 256, 128), BF),
    b_pk=((4, 256, 128), BF),
    b_es=((4, 384, 128), BF),
    b_er=((4, 384, 128), BF),
    b_exs=((3, 384, 128), BF),
    b_exr=((3, 384, 128), BF),
    b_pbs=((64, 768), F32),
    b_pb=((384, 128), F32),
    b_g=((4, 2, 2, 384, 128), BF),
    b_hs=((3, 384, 128), BF),
    b_hr=((3, 384, 128), BF),
    b_fx=((512, 128), BF),
    b_v=((2, 4, 2, 256, 128), BF),
    b_vr=((2, 4, 256, 128), BF),
    b_vxs=((7, 256, 128), BF),
    b_vxr=((7, 256, 128), BF),
    b_ck=((4, 256, 128), BF),
    b_ls=((4, 512, 128), BF),
    b_k=((4, 512, 128), F32),
    b_lr=((4, 512, 128), BF),
    b_lxs=((3, 512, 128), BF),
    b_lxr=((3, 512, 128), BF),
    b_cbs=((64, 1024), F32),
    b_cb=((512, 128), F32),
    b_h=((4, 2, 512, 128), BF),
    b_ms=((3, 512, 128), BF),
    b_mr=((3, 512, 128), BF),
)
N_REMOTE = 320
ORDER = "BFBFBFBFBBFFBFBBFBFBFFBBFBFFBFBBFBFBFFBBFBF"
N_LOCAL = len(INPUTS) + len(OUTPUTS)


def dot(a, b):
    return jnp.dot(a, b, preferred_element_type=F32)


def dot_t(a, b):
    return lax.dot_general(a, b, (((0,), (0,)), ((), ())), preferred_element_type=F32)


def body(*refs):
    n_in, n_out = len(INPUTS), len(OUTPUTS)
    hbm_in = refs[:n_in]
    hbm_out = refs[n_in : n_in + n_out]
    rest = refs[n_in + n_out :]
    names = [*INPUTS, *OUTPUTS, *SCRATCH]
    v = types.SimpleNamespace(**dict(zip(names, rest)))
    send_sems, recv_sems, local_sems = rest[len(names) :]

    sec = lax.axis_index("sec")
    row = lax.axis_index("row")
    z = lax.axis_index("col")
    x = row // 2
    c = row % 2
    sib = 1 - c
    h = sec % 2
    p = sec // 2
    oh = 1 - h

    def at_x(d):
        return {"row": ((x + d) % 4) * 2 + c}

    def at_y(d):
        return {"sec": (sec + d) % 4}

    def at_z(d):
        return {"col": (z + d) % 4}

    def at_xy(dx, dy):
        return {"row": ((x + dx) % 4) * 2 + c, "sec": (sec + dy) % 4}

    def at_px(d, q):
        return {"row": ((x + d) % 4) * 2 + c, "sec": p * 2 + (oh if q else h)}

    def at_pz(d, q):
        return {"col": (z + d) % 4, "sec": p * 2 + (oh if q else h)}

    sibling = {"row": x * 2 + sib}
    near = (0, 1, 3, 2)
    eight = [(0, 1)] + [(d, q) for d in (1, 3, 2) for q in (0, 1)]

    loads = {}
    for i, (ref, src) in enumerate(zip(rest, hbm_in)):
        if len(src.shape) > len(ref.shape):
            src = src.at[0]
        loads[id(ref)] = pltpu.make_async_copy(src, ref, local_sems.at[i])
    first = (v.i_rb, v.i_cr, v.i_cb, v.i_pb, v.wci, v.wr, v.cmap, v.pmap)
    for ref in first + (v.wcl, v.i_pr, v.wpi, v.wpl, v.i_rr):
        loads[id(ref)].start()

    def need(*wanted):
        for ref in wanted:
            copy = loads.pop(id(ref), None)
            if copy is not None:
                copy.wait()

    stores = []

    def emit(ref, i):
        dst = hbm_out[i]
        if len(dst.shape) > 2:
            dst = dst.at[0]
        copy = pltpu.make_async_copy(ref, dst, local_sems.at[n_in + i])
        copy.start()
        stores.append(copy)

    barrier = pltpu.get_barrier_semaphore()
    peers = [sibling] + [at_z(d) for d in (1, 2, 3)] + [at_pz(d, 1) for d in (1, 2, 3)]
    peers += [at_xy(dx, dy) for dx in range(4) for dy in range(4) if dx or dy]
    for peer in peers:
        pl.semaphore_signal(barrier, inc=1, device_id=peer, device_id_type=MESH)
    pl.semaphore_wait(barrier, len(peers))

    sent = []

    def send(src, dst, peer):
        n = len(sent)
        copy = pltpu.make_async_remote_copy(
            src_ref=src,
            dst_ref=dst,
            send_sem=send_sems.at[n],
            recv_sem=recv_sems.at[n],
            device_id=peer,
            device_id_type=MESH,
        )
        copy.start()
        sent.append(copy)
        return copy

    def arrive(copies):
        for copy in copies:
            copy.wait_recv()

    def spread(ref, where):
        return [send(ref, ref, where(d)) for d in (1, 3, 2)]

    def lanes(full):
        turned = full.T
        return jnp.where(c == 0, turned[:64], turned[64:])

    def both(mine, other):
        first = jnp.where(c == 0, mine, other)
        second = jnp.where(c == 0, other, mine)
        return jnp.concatenate([first, second], axis=0).T

    def tiles(count, size):
        def wrap(step):
            @pl.loop(0, count // size)
            def _(i):
                step(pl.ds(pl.multiple_of(i * size, size), size))

        return wrap

    def slot(d, q):
        return 3 + d if q else d - 1

    def tot7(part, m):
        return tot(part, m) + (
            (part[3, m, :].astype(F32) + part[4, m, :].astype(F32))
            + (part[5, m, :].astype(F32) + part[6, m, :].astype(F32))
        )

    def hand_over(ref, got):
        core = []
        for d in near:
            arrive(got[d])
            part = ref((x + 4 - d) % 4)
            core.append(send(part, part, sibling))
        return core

    def exchange(targets, buf, land, finish, home, onward, core):
        size = home.shape[0] // 2
        tile = 128 if size % 128 == 0 else 96
        first, found = [], []
        for half in range(2):
            at = pl.ds(half * size, size)
            got = []
            for k, keep, part, peer in targets:
                hand_on(keep.at[at], part.at[at], buf.at[k, at], size)
                got.append(send(buf.at[k, at], land.at[k, at], peer))
            first.append(got)
        yield
        for half in range(2):
            at = pl.ds(half * size, size)
            arrive(first[half])

            @tiles(size, tile)
            def _(m):
                finish(pl.ds(pl.multiple_of(half * size + m.start, tile), tile))

            ref = home.at[at]
            for peer, where in onward:
                found.append((send(ref, ref, peer), where.at[at]))
            core.append(send(ref, ref, sibling))
        yield
        for copy, where in found:
            copy.wait_recv()
            core.append(send(where, where, sibling))
        yield

    def select(core, matrix, src, out):
        rows = matrix.shape[0]
        for i, d in enumerate(near):
            core[i].wait_recv()
            ch = (x + 4 - d) % 4
            for q in range(2):
                at = pl.ds(pl.multiple_of(q * 2048 + ch * 512, 512), 512)
                r = dot(matrix[:, at], src[q, pl.ds(2 * ch, 2)].reshape(512, 128))
                if i == 0 and q == 0:
                    out[:rows, :] = r
                else:
                    out[:rows, :] = out[:rows, :] + r

    def build(ref, base_of, table, first):
        count = ref.shape[0]

        @pl.loop(0, 16)
        def _(k):
            at = pl.multiple_of(lax.rem(k, 8) * 256, 256)
            part = table[pl.ds(first + k // 8, 1), pl.ds(at, 256)]
            for lo in range(0, count, 128):
                target = base_of(lax.broadcasted_iota(I32, (128, 256), 0) + lo)
                hit = jnp.where(jnp.broadcast_to(part, (128, 256)) == target, 1.0, 0.0)
                ref[lo : lo + 128, pl.ds(pl.multiple_of(k * 256, 256), 256)] = hit.astype(BF)

    def wide(src, depth):
        parts = [src[j].reshape(depth, 128) for j in range(4)]
        return jnp.concatenate(parts, axis=1)

    def back_mm(w, start, src, depth, out):
        at = pl.ds(pl.multiple_of(start, 128), out.shape[1])
        r = dot_t(w[:, at], wide(src, depth))
        for j in range(4):
            out[j] = r[:, j * 128 : (j + 1) * 128].astype(out.dtype)

    def pick(matrix, vec, out, part):
        core = []
        for q in range(2):

            @pl.loop(0, 4)
            def _(k):
                at = pl.multiple_of(q * 2048 + k * 512, 512)
                r = dot_t(matrix[:, pl.ds(at, 512)], vec[...])
                out[q, k] = r.astype(BF).reshape(2, 256, 128)

            core.append(send(out.at[q, :, sib], part.at[q], sibling))
        return core

    def hand_on(keep, part, buf, count):
        @tiles(count, 128 if count % 128 == 0 else 96)
        def _(m):
            buf[m, :] = (keep[m, :] + part[m, :].astype(F32)).astype(BF)

    def tot(part, m):
        return (part[0, m, :].astype(F32) + part[1, m, :].astype(F32)) + part[2, m, :].astype(F32)

    def root_sum(s, k, lo):
        mine = v.f_t[c, s, k, :, lo : lo + 256].astype(F32)
        return mine + v.f_tr[s, k, :, lo : lo + 256].astype(F32)

    def child_base(j):
        return jnp.where(
            j < 384, h * 3072 + row * 384 + j, 6144 - 384 + row * 256 + h * 128 + j
        )

    def root_base(j):
        return (sec * 8 + row) * 384 + j

    def forward():
        need(v.i_cr)
        v.f_x[z] = v.i_cr[...].astype(BF)
        got = spread(v.f_x.at[z], at_z)
        yield
        need(v.cmap)
        build(v.sel, child_base, v.cmap, 2 * p)
        need(v.wci)
        core = []
        order = (0, 1, 3, 2)
        for d in order:
            if d:
                got[order.index(d) - 1].wait_recv()
            ch = (z + 4 - d) % 4
            v.f_ps[ch] = dot(v.wci[pl.ds(sib * 512, 512), :], v.f_x[ch]).astype(BF)
            core.append(send(v.f_ps.at[ch], v.f_pr.at[ch], sibling))
        for ch in range(4):
            v.f_k[ch, :512] = dot(v.wci[pl.ds(c * 512, 512), :], v.f_x[ch])
        yield
        arrive(core)

        def finish(m):
            own = (v.f_k[x, m, :] + v.f_pr[x, m, :].astype(F32)) + tot(v.f_xr, m)
            v.f_x2[x, c, m, :] = own.astype(BF)
            v.f_u[m, :] = own

        core = []
        yield from exchange(
            [
                (d - 1, v.f_k.at[(x + d) % 4], v.f_pr.at[(x + d) % 4], at_x(d))
                for d in (1, 3, 2)
            ],
            v.f_xs,
            v.f_xr,
            finish,
            v.f_x2.at[x, c],
            [(at_x(d), v.f_x2.at[(x + 4 - d) % 4, c]) for d in (1, 3, 2)],
            core,
        )
        up = send(v.f_u, v.f_us, sibling)
        need(v.wcl)
        arrive(core)
        got = []
        for d in (1, 3, 2):
            ch = (z + d) % 4
            r = dot(v.wcl[...], v.f_x2[ch].reshape(1024, 128))
            v.f_cs[d - 1] = r.astype(BF)
            got.append(send(v.f_cs.at[d - 1], v.f_cr.at[d - 1], at_z(d)))
        own = dot(v.wcl[...], v.f_x2[z].reshape(1024, 128))
        yield
        arrive(got)
        own = own + (v.f_cr[0].astype(F32) + v.f_cr[1].astype(F32)) + v.f_cr[2].astype(F32)
        v.f_c[h, row] = (-own).astype(BF)
        got = {d: [] for d in near}
        for d, q in eight:
            got[d].append(send(v.f_c.at[h, row], v.f_c.at[h, row], at_px(d, q)))
        up.wait_recv()
        v.o_cu[:, pl.ds(pl.multiple_of(c * 512, 128), 512)] = lanes(v.f_u[...])
        v.o_cu[:, pl.ds(pl.multiple_of(sib * 512, 128), 512)] = lanes(v.f_us[...])
        emit(v.o_cu, 0)
        yield
        need(v.i_pr)
        core = hand_over(lambda k: v.f_c.at[:, 2 * k + c], got)
        yield
        select(core, v.sel, v.f_c, v.f_fr)

        @tiles(384, 128)
        def _(m):
            v.f_px[z, m, :] = (v.i_pr[m, :] + v.f_fr[m, :]).astype(BF)

        got = spread(v.f_px.at[z], at_z)
        yield
        need(v.wpi)
        core = []
        for d in order:
            if d:
                got[order.index(d) - 1].wait_recv()
            ch = (z + 4 - d) % 4
            for half in range(2):
                w = v.wpi[pl.ds(half * 768 + sib * 384, 384), :]
                v.f_qs[ch, half * 384 : (half + 1) * 384] = dot(w, v.f_px[ch]).astype(BF)
            core.append(send(v.f_qs.at[ch], v.f_qr.at[ch], sibling))
        for ch in range(4):
            for half in range(2):
                w = v.wpi[pl.ds(half * 768 + c * 384, 384), :]
                v.f_k[ch, half * 384 : (half + 1) * 384] = dot(w, v.f_px[ch])
        yield
        arrive(core)

        def finish(m):
            at = pl.ds(pl.multiple_of(h * 384 + m.start, 32), m.size)
            own = v.f_k[x, at, :] + v.f_qr[x, at, :].astype(F32) + tot7(v.f_qxr, m)
            v.f_pu[m, :] = own
            v.f_x3[x, c, m, :] = own.astype(BF)

        core = []
        targets = []
        for d, q in eight[1:] + eight[:1]:
            ch = (x + d) % 4
            at = pl.ds(pl.multiple_of((oh if q else h) * 384, 128), 384)
            targets.append((slot(d, q), v.f_k.at[ch, at], v.f_qr.at[ch, at], at_px(d, q)))
        yield from exchange(
            targets,
            v.f_qxs,
            v.f_qxr,
            finish,
            v.f_x3.at[x, c],
            [(at_x(d), v.f_x3.at[(x + 4 - d) % 4, c]) for d in (1, 3, 2)],
            core,
        )
        up = send(v.f_pu, v.f_pus, sibling)
        need(v.wpl)
        arrive(core)
        got = []
        for d in (1, 3, 2, 0):
            ch = (z + d) % 4
            v.f_uk[ch] = dot(v.wpl[...], v.f_x3[ch].reshape(768, 128))
            for q in (0, 1):
                if d or q:
                    at = pl.ds(pl.multiple_of((oh if q else h) * 128, 128), 128)
                    v.f_ds[slot(d, q)] = v.f_uk[ch, at, :].astype(BF)
                    got.append(send(v.f_ds.at[slot(d, q)], v.f_dr.at[slot(d, q)], at_pz(d, q)))
        up.wait_recv()
        v.o_pu[:, pl.ds(pl.multiple_of(c * 384, 128), 384)] = lanes(v.f_pu[...])
        v.o_pu[:, pl.ds(pl.multiple_of(sib * 384, 128), 384)] = lanes(v.f_pus[...])
        emit(v.o_pu, 1)
        yield
        arrive(got)
        own = v.f_uk[z, pl.ds(h * 128, 128), :] + tot7(v.f_dr, slice(None))
        v.f_r[p, row, h] = (v.f_fr[384:, :] - own).astype(BF)
        got = {d: [] for d in near}
        for dx in near:
            for dy in near:
                if dx or dy:
                    ref = v.f_r.at[p, row, h]
                    got[dx].append(send(ref, ref, at_xy(dx, dy)))
        yield
        need(v.i_rr)
        core = hand_over(lambda k: v.f_r.at[:, 2 * k + c], got)
        yield
        select(core, v.rsel, v.f_r, v.f_fr)

        @tiles(384, 128)
        def _(m):
            v.f_rx[z, m, :] = (v.i_rr[m, :] + v.f_fr[m, :]).astype(BF)

        got = spread(v.f_rx.at[z], at_z)
        yield
        arrive(got)
        core = []
        for dy in (1, 3, 2, 0):
            s = (sec + dy) % 4

            @pl.loop(0, 2)
            def _(k):
                start = pl.multiple_of(s * 768 + k * 384, 384)
                r = dot(v.wr[pl.ds(start, 384), :], wide(v.f_rx, 384))
                for j in range(2):
                    for cc in range(2):
                        at = (2 * j + cc) * 96
                        v.f_t[cc, s, 2 * k + j] = r[at : at + 96].astype(BF)

            core.append(send(v.f_t.at[sib, s], v.f_tr.at[s], sibling))
        yield
        got_a, got_b = [], []
        for i, dy in enumerate((1, 3, 2, 0)):
            s = (sec + dy) % 4
            core[i].wait_recv()
            if dy:

                @pl.loop(0, 4)
                def _(k):
                    v.f_bs[dy - 1, k] = root_sum(s, k, 256).astype(BF)

                got_b.append(send(v.f_bs.at[dy - 1], v.f_br.at[dy - 1], at_y(dy)))
            else:

                @pl.loop(0, 4)
                def _(k):
                    v.f_ob[k] = root_sum(s, k, 256)

            part = []
            for d in (1, 3, 2):
                v.f_as[d - 1, s] = root_sum(s, (x + d) % 4, 0).astype(BF)
                part.append(send(v.f_as.at[d - 1, s], v.f_ar.at[d - 1, s], at_x(d)))
            got_a.append(part)
            v.f_oa[s] = root_sum(s, x, 0)
        yield

        def gathered(total, part, k):
            return total[k] + (
                (part[0, k].astype(F32) + part[1, k].astype(F32)) + part[2, k].astype(F32)
            )

        got = []
        for i, dy in enumerate((1, 3, 2, 0)):
            s = (sec + dy) % 4
            arrive(got_a[i])
            if dy:
                v.f_a2s[dy - 1] = gathered(v.f_oa, v.f_ar, s).astype(BF)
                got.append(send(v.f_a2s.at[dy - 1], v.f_a2r.at[dy - 1], at_y(dy)))
            else:
                v.f_oa[s] = gathered(v.f_oa, v.f_ar, s)
        arrive(got_b)
        for d in (1, 3, 2):
            v.f_b2s[d - 1] = gathered(v.f_ob, v.f_br, (x + d) % 4).astype(BF)
            got.append(send(v.f_b2s.at[d - 1], v.f_b2r.at[d - 1], at_x(d)))
        v.f_ob[x] = gathered(v.f_ob, v.f_br, x)
        yield
        arrive(got)
        for total, me, part, lo in ((v.f_oa, sec, v.f_a2r, 0), (v.f_ob, x, v.f_b2r, 256)):
            v.o_ru[:, lo : lo + 256] = total[me] + (
                (part[0].astype(F32) + part[1].astype(F32)) + part[2].astype(F32)
            )
        emit(v.o_ru, 2)

    def backward():
        need(v.i_rb)
        v.b_y[sec, x, c] = v.i_rb[...].astype(BF)
        got_x = spread(v.b_y.at[sec, x, c], at_x)
        got_y = spread(v.b_y.at[sec, x, c], at_y)
        need(v.i_cb, v.i_pb)
        cbs = send(v.i_cb, v.b_cbs, sibling)
        pbs = send(v.i_pb, v.b_pbs, sibling)
        yield
        need(v.pmap)
        build(v.rsel, root_base, v.pmap, 0)
        got_a, got_b = [], []
        for i, d in enumerate((1, 3, 2)):
            got_x[i].wait_recv()
            got_a.append(spread(v.b_y.at[sec, (x + 4 - d) % 4, c, :, 0:256], at_y))
            got_y[i].wait_recv()
            got_b.append(spread(v.b_y.at[(sec + 4 - d) % 4, x, c, :, 256:512], at_x))
        core = [send(v.b_y.at[sec, :, c], v.b_y.at[sec, :, c], sibling)]
        yield
        for i, d in enumerate((1, 3, 2)):
            arrive([part[i] for part in got_a])
            arrive(got_b[i])
            ref = v.b_y.at[(sec + 4 - d) % 4, :, c]
            core.append(send(ref, ref, sibling))
        need(v.wr)
        yield
        for i, d in enumerate(near):
            core[i].wait_recv()
            s = (sec + 4 - d) % 4

            w = v.wr[pl.ds(pl.multiple_of(s * 768, 768), 768), :]
            r = dot_t(w, v.b_y[s].reshape(768, 512))
            for j in range(4):
                part = r[:, j * 128 : (j + 1) * 128]
                v.b_r[j] = part if i == 0 else v.b_r[j] + part

        got = []
        for d in (1, 3, 2):
            v.b_rs[d - 1] = v.b_r[(z + d) % 4].astype(BF)
            got.append(send(v.b_rs.at[d - 1], v.b_rr.at[d - 1], at_z(d)))
        yield
        arrive(got)

        @tiles(384, 128)
        def _(m):
            own = v.b_r[z, m, :] + tot(v.b_rr, m)
            v.o_rx[m, :] = own
            v.b_rx[m, :] = own.astype(BF)

        emit(v.o_rx, 5)
        core = pick(v.rsel, v.b_rx, v.b_t, v.b_tr)
        yield
        arrive(core)
        got = []
        for d in (1, 3, 2):
            ch = (x + d) % 4
            for q in range(2):
                v.b_txs[d - 1, q] = v.b_t[q, ch, c] + v.b_tr[q, ch]
            got.append(send(v.b_txs.at[d - 1], v.b_txr.at[d - 1], at_x(d)))
        yield
        arrive(got)
        for q in range(2):
            own = v.b_t[q, x, c] + v.b_tr[q, x]
            v.b_tp[q] = own + ((v.b_txr[0, q] + v.b_txr[1, q]) + v.b_txr[2, q])
        got = []
        for d in (1, 3, 2):
            got.append(send(v.b_tp.at[((sec + d) % 4) // 2], v.b_tpr.at[d - 1], at_y(d)))
        yield
        arrive(got)
        v.b_pk[z] = v.b_tp[p] + ((v.b_tpr[0] + v.b_tpr[1]) + v.b_tpr[2])
        got = spread(v.b_pk.at[z], at_z)
        yield
        need(v.wpl)
        arrive(got)
        back_mm(v.wpl, sib * 384, v.b_pk, 256, v.b_es)
        core = [send(v.b_es, v.b_er, sibling)]
        back_mm(v.wpl, c * 384, v.b_pk, 256, v.b_k.at[:, :384])
        yield
        arrive(core)

        def finish(m):
            own = v.b_k[x, m, :] + v.b_er[x, m, :].astype(F32)
            own = v.b_pb[m, :] - (own + tot(v.b_exr, m))
            v.b_g[x, h, c, m, :] = own.astype(BF)

        core = []
        pbs.wait_recv()
        at = pl.ds(pl.multiple_of(c * 384, 128), 384)
        v.b_pb[...] = both(v.i_pb[:, at], v.b_pbs[:, at])
        yield from exchange(
            [
                (d - 1, v.b_k.at[(x + d) % 4, :384], v.b_er.at[(x + d) % 4], at_x(d))
                for d in (1, 3, 2)
            ],
            v.b_exs,
            v.b_exr,
            finish,
            v.b_g.at[x, h, c],
            [
                (at_px(d, q), v.b_g.at[(x + 4 - d) % 4, oh if q else h, c])
                for d, q in eight[1:] + eight[:1]
            ],
            core,
        )
        need(v.wpi)
        arrive(core)
        back_mm(v.wpi, 0, v.b_g, 1536, v.b_r)
        got = []
        for d in (1, 3, 2):
            v.b_hs[d - 1] = v.b_r[(z + d) % 4].astype(BF)
            got.append(send(v.b_hs.at[d - 1], v.b_hr.at[d - 1], at_z(d)))
        yield
        arrive(got)

        @tiles(384, 128)
        def _(m):
            own = v.b_r[z, m, :] + tot(v.b_hr, m)
            v.o_px[m, :] = own
            v.b_fx[m, :] = own.astype(BF)

        emit(v.o_px, 4)
        v.b_fx[384:, :] = v.b_pk[z, pl.ds(h * 128, 128), :]
        core = pick(v.sel, v.b_fx, v.b_v, v.b_vr)
        yield
        arrive(core)
        got = []
        for d, q in eight[1:] + eight[:1]:
            ch = (x + d) % 4
            a = oh if q else h
            v.b_vxs[slot(d, q)] = v.b_v[a, ch, c] + v.b_vr[a, ch]
            got.append(send(v.b_vxs.at[slot(d, q)], v.b_vxr.at[slot(d, q)], at_px(d, q)))
        yield
        arrive(got)
        own = v.b_v[h, x, c] + v.b_vr[h, x] + (v.b_vxr[0] + v.b_vxr[1] + v.b_vxr[2])
        own = own + ((v.b_vxr[3] + v.b_vxr[4]) + (v.b_vxr[5] + v.b_vxr[6]))
        v.b_ck[z] = own
        got = spread(v.b_ck.at[z], at_z)
        yield
        need(v.wcl)
        arrive(got)
        back_mm(v.wcl, sib * 512, v.b_ck, 256, v.b_ls)
        core = [send(v.b_ls, v.b_lr, sibling)]
        back_mm(v.wcl, c * 512, v.b_ck, 256, v.b_k)
        yield
        arrive(core)

        def finish(m):
            own = v.b_k[x, m, :] + v.b_lr[x, m, :].astype(F32)
            own = v.b_cb[m, :] - (own + tot(v.b_lxr, m))
            v.b_h[x, c, m, :] = own.astype(BF)

        core = []
        cbs.wait_recv()
        at = pl.ds(pl.multiple_of(c * 512, 128), 512)
        v.b_cb[...] = both(v.i_cb[:, at], v.b_cbs[:, at])
        yield from exchange(
            [
                (d - 1, v.b_k.at[(x + d) % 4], v.b_lr.at[(x + d) % 4], at_x(d))
                for d in (1, 3, 2)
            ],
            v.b_lxs,
            v.b_lxr,
            finish,
            v.b_h.at[x, c],
            [(at_x(d), v.b_h.at[(x + 4 - d) % 4, c]) for d in (1, 3, 2)],
            core,
        )
        need(v.wci)
        arrive(core)
        back_mm(v.wci, 0, v.b_h, 1024, v.b_k)
        got = []
        for d in (1, 3, 2):
            v.b_ms[d - 1] = v.b_k[(z + d) % 4].astype(BF)
            got.append(send(v.b_ms.at[d - 1], v.b_mr.at[d - 1], at_z(d)))
        yield
        arrive(got)

        @tiles(512, 128)
        def _(m):
            v.o_cx[m, :] = v.b_k[z, m, :] + tot(v.b_mr, m)

        emit(v.o_cx, 3)

    chains = dict(B=backward(), F=forward())
    for name in ORDER + "BF" * 60:
        if name in chains:
            try:
                next(chains[name])
            except StopIteration:
                del chains[name]
    for copy in loads.values():
        copy.wait()
    for copy in sent:
        copy.wait_send()
    for copy in stores:
        copy.wait()


def write_out(*refs):
    n = len(OUTPUTS)
    stage, sems = refs[2 * n : 3 * n], refs[3 * n]
    loads = [pltpu.make_async_copy(refs[i], stage[i], sems.at[0, i]) for i in range(n)]
    for copy in loads:
        copy.start()
    stores = [pltpu.make_async_copy(stage[i], refs[n + i], sems.at[1, i]) for i in range(n)]
    for load, store in zip(loads, stores):
        load.wait()
        store.start()
    for store in stores:
        store.wait()


def per_device(*args):
    any_space = pl.BlockSpec(memory_space=pl.ANY)
    shapes = (
        (1, 64, 1024),
        (1, 64, 768),
        (1, 96, 512),
        (1, 512, 128),
        (1, 384, 128),
        (384, 128),
    )
    scratch = [pltpu.VMEM(s, t) for part in (INPUTS, OUTPUTS, SCRATCH) for s, t in part.values()]
    scratch += [
        pltpu.SemaphoreType.DMA((N_REMOTE,)),
        pltpu.SemaphoreType.DMA((N_REMOTE,)),
        pltpu.SemaphoreType.DMA((N_LOCAL,)),
    ]
    args = list(args)
    for i in (10, 11):
        args[i] = jnp.swapaxes(args[i], 1, 2)
    outs = pl.pallas_call(
        body,
        out_shape=tuple(jax.ShapeDtypeStruct(s, F32) for s in shapes),
        in_specs=[any_space] * len(INPUTS),
        out_specs=(any_space,) * len(OUTPUTS),
        scratch_shapes=scratch,
        compiler_params=pltpu.CompilerParams(
            collective_id=0, has_side_effects=True, vmem_limit_bytes=63 * 1024 * 1024
        ),
    )(*args)
    outs = pl.pallas_call(
        write_out,
        out_shape=tuple(jax.ShapeDtypeStruct(s, F32) for s in shapes),
        in_specs=[any_space] * len(OUTPUTS),
        out_specs=(any_space,) * len(OUTPUTS),
        scratch_shapes=[pltpu.VMEM(s, F32) for s in shapes]
        + [pltpu.SemaphoreType.DMA((2, len(OUTPUTS)))],
    )(*outs)
    return tuple(jnp.swapaxes(o, 1, 2) if i < 2 else o for i, o in enumerate(outs))


def solution(mesh):
    return jax.shard_map(
        per_device,
        mesh=mesh,
        in_specs=(
            P("sec", "col", "row"),
            P("sec", "row", "col"),
            P("sec", "col", "row"),
            P("sec", "row", "col"),
            P("col", ("sec", "row")),
            P(),
            P(),
            P("sec", "row", "col"),
            P("sec", "row", "col"),
            P(("sec", "row"), "col"),
            P("sec", "col", "row"),
            P("sec", "col", "row"),
            P("col", ("sec", "row"), None),
        ),
        out_specs=(
            P("sec", "col", "row"),
            P("sec", "col", "row"),
            P("col", ("sec", "row"), None),
            P("sec", "row", "col"),
            P("sec", "row", "col"),
            P(("sec", "row"), "col"),
        ),
        check_vma=False,
    )
```

```python
import types

import jax
import jax.numpy as jnp
from jax import lax
from jax.experimental import pallas as pl
from jax.experimental.pallas import tpu as pltpu
from jax.sharding import PartitionSpec as P

BF = jnp.bfloat16
F32 = jnp.float32
I32 = jnp.int32
MESH = pl.DeviceIdType.MESH

INPUTS = dict(
    wci=((1024, 512), BF),
    wcl=((256, 1024), BF),
    wpi=((1536, 384), BF),
    wpl=((256, 768), BF),
    wr=((3072, 384), BF),
    cmap=((4, 2048), I32),
    pmap=((2, 2048), I32),
    i_cr=((512, 128), F32),
    i_pr=((384, 128), F32),
    i_rr=((384, 128), F32),
    i_cb=((64, 1024), F32),
    i_pb=((64, 768), F32),
    i_rb=((96, 512), F32),
)
OUTPUTS = dict(
    o_cu=((64, 1024), F32),
    o_pu=((64, 768), F32),
    o_ru=((96, 512), F32),
    o_cx=((512, 128), F32),
    o_px=((384, 128), F32),
    o_rx=((384, 128), F32),
)
SCRATCH = dict(
    sel=((512, 4096), BF),
    rsel=((384, 4096), BF),
    f_x=((4, 512, 128), BF),
    f_ps=((4, 512, 128), BF),
    f_pr=((4, 512, 128), BF),
    f_xs=((3, 512, 128), BF),
    f_xr=((3, 512, 128), BF),
    f_u=((512, 128), F32),
    f_us=((512, 128), F32),
    f_x2=((4, 2, 512, 128), BF),
    f_cs=((3, 256, 128), BF),
    f_cr=((3, 256, 128), BF),
    f_c=((2, 8, 256, 128), BF),
    f_px=((4, 384, 128), BF),
    f_qs=((4, 768, 128), BF),
    f_k=((4, 768, 128), F32),
    f_qr=((4, 768, 128), BF),
    f_qxs=((7, 384, 128), BF),
    f_qxr=((7, 384, 128), BF),
    f_pu=((384, 128), F32),
    f_pus=((384, 128), F32),
    f_x3=((4, 2, 384, 128), BF),
    f_ds=((7, 128, 128), BF),
    f_dr=((7, 128, 128), BF),
    f_uk=((4, 256, 128), F32),
    f_fr=((512, 128), F32),
    f_r=((2, 8, 2, 128, 128), BF),
    f_rx=((4, 384, 128), BF),
    f_t=((2, 4, 4, 96, 512), BF),
    f_tr=((4, 4, 96, 512), BF),
    f_as=((3, 4, 96, 256), BF),
    f_bs=((3, 4, 96, 256), BF),
    f_ar=((3, 4, 96, 256), BF),
    f_br=((3, 4, 96, 256), BF),
    f_oa=((4, 96, 256), F32),
    f_ob=((4, 96, 256), F32),
    f_a2s=((3, 96, 256), BF),
    f_b2s=((3, 96, 256), BF),
    f_a2r=((3, 96, 256), BF),
    f_b2r=((3, 96, 256), BF),
    b_y=((4, 4, 2, 96, 512), BF),
    b_r=((4, 384, 128), F32),
    b_rs=((3, 384, 128), BF),
    b_rr=((3, 384, 128), BF),
    b_rx=((384, 128), BF),
    b_t=((2, 4, 2, 256, 128), BF),
    b_tr=((2, 4, 256, 128), BF),
    b_txs=((3, 2, 256, 128), BF),
    b_txr=((3, 2, 256, 128), BF),
    b_tp=((2, 256, 128), BF),
    b_tpr=((3, 256, 128), BF),
    b_pk=((4, 256, 128), BF),
    b_es=((4, 384, 128), BF),
    b_er=((4, 384, 128), BF),
    b_exs=((3, 384, 128), BF),
    b_exr=((3, 384, 128), BF),
    b_pbs=((64, 768), F32),
    b_pb=((384, 128), F32),
    b_g=((4, 2, 2, 384, 128), BF),
    b_hs=((3, 384, 128), BF),
    b_hr=((3, 384, 128), BF),
    b_fx=((512, 128), BF),
    b_v=((2, 4, 2, 256, 128), BF),
    b_vr=((2, 4, 256, 128), BF),
    b_vxs=((7, 256, 128), BF),
    b_vxr=((7, 256, 128), BF),
    b_vo=((256, 128), BF),
    b_ck=((4, 256, 128), BF),
    b_ls=((4, 512, 128), BF),
    b_k=((4, 512, 128), F32),
    b_lr=((4, 512, 128), BF),
    b_lxs=((3, 512, 128), BF),
    b_lxr=((3, 512, 128), BF),
    b_cbs=((64, 1024), F32),
    b_cb=((512, 128), F32),
    b_h=((4, 2, 512, 128), BF),
    b_ms=((3, 512, 128), BF),
    b_mr=((3, 512, 128), BF),
)
N_REMOTE = 320
ORDER = "BFBFBFBFBBFFBFBBBFFBFFBBFBFFBBFBBFFBFBFBFBF"
N_LOCAL = len(INPUTS) + len(OUTPUTS)


def dot(a, b):
    return jnp.dot(a, b, preferred_element_type=F32)


def dot_t(a, b):
    return lax.dot_general(a, b, (((0,), (0,)), ((), ())), preferred_element_type=F32)


def body(*refs):
    n_in, n_out = len(INPUTS), len(OUTPUTS)
    hbm_in = refs[:n_in]
    hbm_out = refs[n_in : n_in + n_out]
    rest = refs[n_in + n_out :]
    names = [*INPUTS, *OUTPUTS, *SCRATCH]
    v = types.SimpleNamespace(**dict(zip(names, rest)))
    send_sems, recv_sems, local_sems = rest[len(names) :]

    sec = lax.axis_index("sec")
    row = lax.axis_index("row")
    z = lax.axis_index("col")
    x = row // 2
    c = row % 2
    sib = 1 - c
    h = sec % 2
    p = sec // 2
    oh = 1 - h

    def at_x(d):
        return {"row": ((x + d) % 4) * 2 + c}

    def at_y(d):
        return {"sec": (sec + d) % 4}

    def at_z(d):
        return {"col": (z + d) % 4}

    def at_xy(dx, dy):
        return {"row": ((x + dx) % 4) * 2 + c, "sec": (sec + dy) % 4}

    def at_px(d, q):
        return {"row": ((x + d) % 4) * 2 + c, "sec": p * 2 + (oh if q else h)}

    def at_pz(d, q):
        return {"col": (z + d) % 4, "sec": p * 2 + (oh if q else h)}

    sibling = {"row": x * 2 + sib}
    near = (0, 1, 3, 2)
    eight = [(0, 1)] + [(d, q) for d in (1, 3, 2) for q in (0, 1)]

    loads = {}
    for i, (ref, src) in enumerate(zip(rest, hbm_in)):
        if len(src.shape) > len(ref.shape):
            src = src.at[0]
        loads[id(ref)] = pltpu.make_async_copy(src, ref, local_sems.at[i])
    first = (v.i_rb, v.i_cr, v.i_cb, v.i_pb, v.wci, v.wr, v.cmap, v.pmap)
    for ref in first + (v.wcl, v.i_pr, v.wpi, v.wpl, v.i_rr):
        loads[id(ref)].start()

    def need(*wanted):
        for ref in wanted:
            copy = loads.pop(id(ref), None)
            if copy is not None:
                copy.wait()

    stores = []

    def emit(ref, i):
        dst = hbm_out[i]
        if len(dst.shape) > 2:
            dst = dst.at[0]
        copy = pltpu.make_async_copy(ref, dst, local_sems.at[n_in + i])
        copy.start()
        stores.append(copy)

    barrier = pltpu.get_barrier_semaphore()
    peers = [sibling] + [at_z(d) for d in (1, 2, 3)] + [at_pz(d, 1) for d in (1, 2, 3)]
    peers += [at_xy(dx, dy) for dx in range(4) for dy in range(4) if dx or dy]
    for peer in peers:
        pl.semaphore_signal(barrier, inc=1, device_id=peer, device_id_type=MESH)
    pl.semaphore_wait(barrier, len(peers))

    sent = []

    def send(src, dst, peer):
        n = len(sent)
        copy = pltpu.make_async_remote_copy(
            src_ref=src,
            dst_ref=dst,
            send_sem=send_sems.at[n],
            recv_sem=recv_sems.at[n],
            device_id=peer,
            device_id_type=MESH,
        )
        copy.start()
        sent.append(copy)
        return copy

    def arrive(copies):
        for copy in copies:
            copy.wait_recv()

    def spread(ref, where):
        return [send(ref, ref, where(d)) for d in (1, 3, 2)]

    def lanes(full):
        turned = full.T
        return jnp.where(c == 0, turned[:64], turned[64:])

    def both(mine, other):
        first = jnp.where(c == 0, mine, other)
        second = jnp.where(c == 0, other, mine)
        return jnp.concatenate([first, second], axis=0).T

    def tiles(count, size):
        def wrap(step):
            @pl.loop(0, count // size)
            def _(i):
                step(pl.ds(pl.multiple_of(i * size, size), size))

        return wrap

    def slot(d, q):
        return 3 + d if q else d - 1

    def tot7(part, m):
        return tot(part, m) + (
            (part[3, m, :].astype(F32) + part[4, m, :].astype(F32))
            + (part[5, m, :].astype(F32) + part[6, m, :].astype(F32))
        )

    def hand_over(ref, got):
        core = []
        for d in near:
            arrive(got[d])
            part = ref((x + 4 - d) % 4)
            core.append(send(part, part, sibling))
        return core

    def exchange(targets, buf, land, finish, home, onward, core):
        size = home.shape[0] // 2
        tile = 128 if size % 128 == 0 else 96
        first, found = [], []
        for half in range(2):
            at = pl.ds(half * size, size)
            got = []
            for k, keep, part, peer in targets:
                hand_on(keep.at[at], part.at[at], buf.at[k, at], size)
                got.append(send(buf.at[k, at], land.at[k, at], peer))
            first.append(got)
        yield
        for half in range(2):
            at = pl.ds(half * size, size)
            arrive(first[half])

            @tiles(size, tile)
            def _(m):
                finish(pl.ds(pl.multiple_of(half * size + m.start, tile), tile))

            ref = home.at[at]
            for peer, where in onward:
                found.append((send(ref, ref, peer), where.at[at]))
            core.append(send(ref, ref, sibling))
        yield
        for copy, where in found:
            copy.wait_recv()
            core.append(send(where, where, sibling))
        yield

    def select(core, matrix, src, out):
        rows = matrix.shape[0]
        for i, d in enumerate(near):
            core[i].wait_recv()
            ch = (x + 4 - d) % 4
            for q in range(2):
                at = pl.ds(pl.multiple_of(q * 2048 + ch * 512, 512), 512)
                r = dot(matrix[:, at], src[q, pl.ds(2 * ch, 2)].reshape(512, 128))
                if i == 0 and q == 0:
                    out[:rows, :] = r
                else:
                    out[:rows, :] = out[:rows, :] + r

    def build(ref, base_of, table, first):
        count = ref.shape[0]

        @pl.loop(0, 16)
        def _(k):
            at = pl.multiple_of(lax.rem(k, 8) * 256, 256)
            part = table[pl.ds(first + k // 8, 1), pl.ds(at, 256)]
            for lo in range(0, count, 128):
                target = base_of(lax.broadcasted_iota(I32, (128, 256), 0) + lo)
                hit = jnp.where(jnp.broadcast_to(part, (128, 256)) == target, 1.0, 0.0)
                ref[lo : lo + 128, pl.ds(pl.multiple_of(k * 256, 256), 256)] = hit.astype(BF)

    def wide(src, depth):
        parts = [src[j].reshape(depth, 128) for j in range(4)]
        return jnp.concatenate(parts, axis=1)

    def back_mm(w, start, src, depth, out):
        at = pl.ds(pl.multiple_of(start, 128), out.shape[1])
        r = dot_t(w[:, at], wide(src, depth))
        for j in range(4):
            out[j] = r[:, j * 128 : (j + 1) * 128].astype(out.dtype)

    def pick(matrix, vec, out, part, give):
        core = []
        order = (1, 3, 2, 0)
        for i, d in enumerate(order):
            ch = (x + d) % 4

            @pl.loop(0, 2)
            def _(q):
                at = pl.multiple_of(q * 2048 + ch * 512, 512)
                r = dot_t(matrix[:, pl.ds(at, 512)], vec[...])
                out[q, ch] = r.astype(BF).reshape(2, 256, 128)

            core.append(send(out.at[:, ch, sib], part.at[:, ch], sibling))
            if i:
                core[i - 1].wait_recv()
                give(order[i - 1])
        yield
        core[3].wait_recv()
        give(0)

    def hand_on(keep, part, buf, count):
        @tiles(count, 128 if count % 128 == 0 else 96)
        def _(m):
            buf[m, :] = (keep[m, :] + part[m, :].astype(F32)).astype(BF)

    def tot(part, m):
        return (part[0, m, :].astype(F32) + part[1, m, :].astype(F32)) + part[2, m, :].astype(F32)

    def root_sum(s, k, lo):
        mine = v.f_t[c, s, k, :, lo : lo + 256].astype(F32)
        return mine + v.f_tr[s, k, :, lo : lo + 256].astype(F32)

    def child_base(j):
        return jnp.where(
            j < 384, h * 3072 + row * 384 + j, 6144 - 384 + row * 256 + h * 128 + j
        )

    def root_base(j):
        return (sec * 8 + row) * 384 + j

    def forward():
        need(v.i_cr)
        v.f_x[z] = v.i_cr[...].astype(BF)
        got = spread(v.f_x.at[z], at_z)
        yield
        need(v.cmap)
        build(v.sel, child_base, v.cmap, 2 * p)
        need(v.wci)
        core = []
        order = (0, 1, 3, 2)
        for d in order:
            if d:
                got[order.index(d) - 1].wait_recv()
            ch = (z + 4 - d) % 4
            v.f_ps[ch] = dot(v.wci[pl.ds(sib * 512, 512), :], v.f_x[ch]).astype(BF)
            core.append(send(v.f_ps.at[ch], v.f_pr.at[ch], sibling))
        for ch in range(4):
            v.f_k[ch, :512] = dot(v.wci[pl.ds(c * 512, 512), :], v.f_x[ch])
        yield
        arrive(core)

        def finish(m):
            own = (v.f_k[x, m, :] + v.f_pr[x, m, :].astype(F32)) + tot(v.f_xr, m)
            v.f_x2[x, c, m, :] = own.astype(BF)
            v.f_u[m, :] = own

        core = []
        yield from exchange(
            [
                (d - 1, v.f_k.at[(x + d) % 4], v.f_pr.at[(x + d) % 4], at_x(d))
                for d in (1, 3, 2)
            ],
            v.f_xs,
            v.f_xr,
            finish,
            v.f_x2.at[x, c],
            [(at_x(d), v.f_x2.at[(x + 4 - d) % 4, c]) for d in (1, 3, 2)],
            core,
        )
        up = send(v.f_u, v.f_us, sibling)
        need(v.wcl)
        arrive(core)
        got = []
        for d in (1, 3, 2):
            ch = (z + d) % 4
            r = dot(v.wcl[...], v.f_x2[ch].reshape(1024, 128))
            v.f_cs[d - 1] = r.astype(BF)
            got.append(send(v.f_cs.at[d - 1], v.f_cr.at[d - 1], at_z(d)))
        own = dot(v.wcl[...], v.f_x2[z].reshape(1024, 128))
        yield
        arrive(got)
        own = own + (v.f_cr[0].astype(F32) + v.f_cr[1].astype(F32)) + v.f_cr[2].astype(F32)
        v.f_c[h, row] = (-own).astype(BF)
        got = {d: [] for d in near}
        for d, q in eight:
            got[d].append(send(v.f_c.at[h, row], v.f_c.at[h, row], at_px(d, q)))
        up.wait_recv()
        v.o_cu[:, pl.ds(pl.multiple_of(c * 512, 128), 512)] = lanes(v.f_u[...])
        v.o_cu[:, pl.ds(pl.multiple_of(sib * 512, 128), 512)] = lanes(v.f_us[...])
        emit(v.o_cu, 0)
        yield
        need(v.i_pr)
        core = hand_over(lambda k: v.f_c.at[:, 2 * k + c], got)
        yield
        select(core, v.sel, v.f_c, v.f_fr)

        @tiles(384, 128)
        def _(m):
            v.f_px[z, m, :] = (v.i_pr[m, :] + v.f_fr[m, :]).astype(BF)

        got = spread(v.f_px.at[z], at_z)
        yield
        need(v.wpi)
        core = []
        for d in order:
            if d:
                got[order.index(d) - 1].wait_recv()
            ch = (z + 4 - d) % 4
            for half in range(2):
                w = v.wpi[pl.ds(half * 768 + sib * 384, 384), :]
                v.f_qs[ch, half * 384 : (half + 1) * 384] = dot(w, v.f_px[ch]).astype(BF)
            core.append(send(v.f_qs.at[ch], v.f_qr.at[ch], sibling))
        for ch in range(4):
            for half in range(2):
                w = v.wpi[pl.ds(half * 768 + c * 384, 384), :]
                v.f_k[ch, half * 384 : (half + 1) * 384] = dot(w, v.f_px[ch])
        yield
        arrive(core)

        def finish(m):
            at = pl.ds(pl.multiple_of(h * 384 + m.start, 32), m.size)
            own = v.f_k[x, at, :] + v.f_qr[x, at, :].astype(F32) + tot7(v.f_qxr, m)
            v.f_pu[m, :] = own
            v.f_x3[x, c, m, :] = own.astype(BF)

        core = []
        targets = []
        for d, q in eight[1:] + eight[:1]:
            ch = (x + d) % 4
            at = pl.ds(pl.multiple_of((oh if q else h) * 384, 128), 384)
            targets.append((slot(d, q), v.f_k.at[ch, at], v.f_qr.at[ch, at], at_px(d, q)))
        yield from exchange(
            targets,
            v.f_qxs,
            v.f_qxr,
            finish,
            v.f_x3.at[x, c],
            [(at_x(d), v.f_x3.at[(x + 4 - d) % 4, c]) for d in (1, 3, 2)],
            core,
        )
        up = send(v.f_pu, v.f_pus, sibling)
        need(v.wpl)
        arrive(core)
        got = []
        for d in (1, 3, 2, 0):
            ch = (z + d) % 4
            v.f_uk[ch] = dot(v.wpl[...], v.f_x3[ch].reshape(768, 128))
            for q in (0, 1):
                if d or q:
                    at = pl.ds(pl.multiple_of((oh if q else h) * 128, 128), 128)
                    v.f_ds[slot(d, q)] = v.f_uk[ch, at, :].astype(BF)
                    got.append(send(v.f_ds.at[slot(d, q)], v.f_dr.at[slot(d, q)], at_pz(d, q)))
        up.wait_recv()
        v.o_pu[:, pl.ds(pl.multiple_of(c * 384, 128), 384)] = lanes(v.f_pu[...])
        v.o_pu[:, pl.ds(pl.multiple_of(sib * 384, 128), 384)] = lanes(v.f_pus[...])
        emit(v.o_pu, 1)
        yield
        arrive(got)
        own = v.f_uk[z, pl.ds(h * 128, 128), :] + tot7(v.f_dr, slice(None))
        v.f_r[p, row, h] = (v.f_fr[384:, :] - own).astype(BF)
        got = {d: [] for d in near}
        for dx in near:
            for dy in near:
                if dx or dy:
                    ref = v.f_r.at[p, row, h]
                    got[dx].append(send(ref, ref, at_xy(dx, dy)))
        yield
        need(v.i_rr)
        core = hand_over(lambda k: v.f_r.at[:, 2 * k + c], got)
        yield
        select(core, v.rsel, v.f_r, v.f_fr)

        @tiles(384, 128)
        def _(m):
            v.f_rx[z, m, :] = (v.i_rr[m, :] + v.f_fr[m, :]).astype(BF)

        got = spread(v.f_rx.at[z], at_z)
        yield
        arrive(got)
        core, got_a, got_b = [], [], []

        def settle(i):
            dy = (1, 3, 2, 0)[i]
            s = (sec + dy) % 4
            core[i].wait_recv()
            if dy:

                @pl.loop(0, 4)
                def _(k):
                    v.f_bs[dy - 1, k] = root_sum(s, k, 256).astype(BF)

                got_b.append(send(v.f_bs.at[dy - 1], v.f_br.at[dy - 1], at_y(dy)))
            else:

                @pl.loop(0, 4)
                def _(k):
                    v.f_ob[k] = root_sum(s, k, 256)

            part = []
            for d in (1, 3, 2):
                v.f_as[d - 1, s] = root_sum(s, (x + d) % 4, 0).astype(BF)
                part.append(send(v.f_as.at[d - 1, s], v.f_ar.at[d - 1, s], at_x(d)))
            got_a.append(part)
            v.f_oa[s] = root_sum(s, x, 0)

        for dy in (1, 3, 2, 0):
            s = (sec + dy) % 4

            @pl.loop(0, 2)
            def _(k):
                start = pl.multiple_of(s * 768 + k * 384, 384)
                r = dot(v.wr[pl.ds(start, 384), :], wide(v.f_rx, 384))
                for j in range(2):
                    for cc in range(2):
                        at = (2 * j + cc) * 96
                        v.f_t[cc, s, 2 * k + j] = r[at : at + 96].astype(BF)

            core.append(send(v.f_t.at[sib, s], v.f_tr.at[s], sibling))
            if len(core) > 1:
                settle(len(core) - 2)
        yield
        settle(3)
        yield

        def gathered(total, part, k):
            return total[k] + (
                (part[0, k].astype(F32) + part[1, k].astype(F32)) + part[2, k].astype(F32)
            )

        got = []
        for i, dy in enumerate((1, 3, 2, 0)):
            s = (sec + dy) % 4
            arrive(got_a[i])
            if dy:
                v.f_a2s[dy - 1] = gathered(v.f_oa, v.f_ar, s).astype(BF)
                got.append(send(v.f_a2s.at[dy - 1], v.f_a2r.at[dy - 1], at_y(dy)))
            else:
                v.f_oa[s] = gathered(v.f_oa, v.f_ar, s)
        arrive(got_b)
        for d in (1, 3, 2):
            v.f_b2s[d - 1] = gathered(v.f_ob, v.f_br, (x + d) % 4).astype(BF)
            got.append(send(v.f_b2s.at[d - 1], v.f_b2r.at[d - 1], at_x(d)))
        v.f_ob[x] = gathered(v.f_ob, v.f_br, x)
        yield
        arrive(got)
        for total, me, part, lo in ((v.f_oa, sec, v.f_a2r, 0), (v.f_ob, x, v.f_b2r, 256)):
            v.o_ru[:, lo : lo + 256] = total[me] + (
                (part[0].astype(F32) + part[1].astype(F32)) + part[2].astype(F32)
            )
        emit(v.o_ru, 2)

    def backward():
        need(v.i_rb)
        v.b_y[sec, x, c] = v.i_rb[...].astype(BF)
        got_x = spread(v.b_y.at[sec, x, c], at_x)
        got_y = spread(v.b_y.at[sec, x, c], at_y)
        need(v.i_cb, v.i_pb)
        cbs = send(v.i_cb, v.b_cbs, sibling)
        pbs = send(v.i_pb, v.b_pbs, sibling)
        yield
        need(v.pmap)
        build(v.rsel, root_base, v.pmap, 0)
        got_a, got_b = [], []
        for i, d in enumerate((1, 3, 2)):
            got_x[i].wait_recv()
            got_a.append(spread(v.b_y.at[sec, (x + 4 - d) % 4, c, :, 0:256], at_y))
            got_y[i].wait_recv()
            got_b.append(spread(v.b_y.at[(sec + 4 - d) % 4, x, c, :, 256:512], at_x))
        core = [send(v.b_y.at[sec, :, c], v.b_y.at[sec, :, c], sibling)]
        yield
        for i, d in enumerate((1, 3, 2)):
            arrive([part[i] for part in got_a])
            arrive(got_b[i])
            ref = v.b_y.at[(sec + 4 - d) % 4, :, c]
            core.append(send(ref, ref, sibling))
        need(v.wr)
        yield
        for i, d in enumerate(near):
            core[i].wait_recv()
            s = (sec + 4 - d) % 4

            w = v.wr[pl.ds(pl.multiple_of(s * 768, 768), 768), :]
            r = dot_t(w, v.b_y[s].reshape(768, 512))
            for j in range(4):
                part = r[:, j * 128 : (j + 1) * 128]
                v.b_r[j] = part if i == 0 else v.b_r[j] + part

        got = []
        for d in (1, 3, 2):
            v.b_rs[d - 1] = v.b_r[(z + d) % 4].astype(BF)
            got.append(send(v.b_rs.at[d - 1], v.b_rr.at[d - 1], at_z(d)))
        yield
        arrive(got)

        @tiles(384, 128)
        def _(m):
            own = v.b_r[z, m, :] + tot(v.b_rr, m)
            v.o_rx[m, :] = own
            v.b_rx[m, :] = own.astype(BF)

        emit(v.o_rx, 5)
        halves = (pl.ds(0, 128), pl.ds(128, 128))
        got = ([], [])

        def give(d):
            ch = (x + d) % 4
            for q in range(2):
                own = v.b_t[q, ch, c] + v.b_tr[q, ch]
                if d:
                    v.b_txs[d - 1, q] = own
                else:
                    v.b_tp[q] = own
            for half, at in enumerate(halves if d else ()):
                src, dst = v.b_txs.at[d - 1, :, at], v.b_txr.at[d - 1, :, at]
                got[half].append(send(src, dst, at_x(d)))

        yield from pick(v.rsel, v.b_rx, v.b_t, v.b_tr, give)
        yield
        got_y = ([], [])
        for half, at in enumerate(halves):
            arrive(got[half])
            for q in range(2):
                found = (v.b_txr[0, q, at] + v.b_txr[1, q, at]) + v.b_txr[2, q, at]
                v.b_tp[q, at] = v.b_tp[q, at] + found
            for d in (1, 3, 2):
                src = v.b_tp.at[((sec + d) % 4) // 2, at]
                got_y[half].append(send(src, v.b_tpr.at[d - 1, at], at_y(d)))
        yield
        got = []
        for half, at in enumerate(halves):
            arrive(got_y[half])
            found = (v.b_tpr[0, at] + v.b_tpr[1, at]) + v.b_tpr[2, at]
            v.b_pk[z, at] = v.b_tp[p, at] + found
            got += spread(v.b_pk.at[z, at], at_z)
        yield
        need(v.wpl)
        arrive(got)
        back_mm(v.wpl, sib * 384, v.b_pk, 256, v.b_es)
        core = [send(v.b_es, v.b_er, sibling)]
        back_mm(v.wpl, c * 384, v.b_pk, 256, v.b_k.at[:, :384])
        yield
        arrive(core)

        def finish(m):
            own = v.b_k[x, m, :] + v.b_er[x, m, :].astype(F32)
            own = v.b_pb[m, :] - (own + tot(v.b_exr, m))
            v.b_g[x, h, c, m, :] = own.astype(BF)

        core = []
        pbs.wait_recv()
        at = pl.ds(pl.multiple_of(c * 384, 128), 384)
        v.b_pb[...] = both(v.i_pb[:, at], v.b_pbs[:, at])
        yield from exchange(
            [
                (d - 1, v.b_k.at[(x + d) % 4, :384], v.b_er.at[(x + d) % 4], at_x(d))
                for d in (1, 3, 2)
            ],
            v.b_exs,
            v.b_exr,
            finish,
            v.b_g.at[x, h, c],
            [
                (at_px(d, q), v.b_g.at[(x + 4 - d) % 4, oh if q else h, c])
                for d, q in eight[1:] + eight[:1]
            ],
            core,
        )
        need(v.wpi)
        arrive(core)
        back_mm(v.wpi, 0, v.b_g, 1536, v.b_r)
        got = []
        for d in (1, 3, 2):
            v.b_hs[d - 1] = v.b_r[(z + d) % 4].astype(BF)
            got.append(send(v.b_hs.at[d - 1], v.b_hr.at[d - 1], at_z(d)))
        yield
        arrive(got)

        @tiles(384, 128)
        def _(m):
            own = v.b_r[z, m, :] + tot(v.b_hr, m)
            v.o_px[m, :] = own
            v.b_fx[m, :] = own.astype(BF)

        emit(v.o_px, 4)
        v.b_fx[384:, :] = v.b_pk[z, pl.ds(h * 128, 128), :]
        got = ([], [])

        def give(d):
            ch = (x + d) % 4
            for q in (0, 1):
                a = oh if q else h
                own = v.b_v[a, ch, c] + v.b_vr[a, ch]
                if d or q:
                    v.b_vxs[slot(d, q)] = own
                else:
                    v.b_vo[...] = own
            for half, at in enumerate(halves):
                for q in (0, 1) if d else (1,):
                    src, dst = v.b_vxs.at[slot(d, q), at], v.b_vxr.at[slot(d, q), at]
                    got[half].append(send(src, dst, at_px(d, q)))

        yield from pick(v.sel, v.b_fx, v.b_v, v.b_vr, give)
        yield
        spreads = []
        for half, at in enumerate(halves):
            arrive(got[half])
            own = v.b_vo[at] + ((v.b_vxr[0, at] + v.b_vxr[1, at]) + v.b_vxr[2, at])
            own = own + (v.b_vxr[3, at] + v.b_vxr[4, at])
            v.b_ck[z, at] = own + (v.b_vxr[5, at] + v.b_vxr[6, at])
            spreads += spread(v.b_ck.at[z, at], at_z)
        got = spreads
        yield
        need(v.wcl)
        arrive(got)
        back_mm(v.wcl, sib * 512, v.b_ck, 256, v.b_ls)
        core = [send(v.b_ls, v.b_lr, sibling)]
        back_mm(v.wcl, c * 512, v.b_ck, 256, v.b_k)
        yield
        arrive(core)

        def finish(m):
            own = v.b_k[x, m, :] + v.b_lr[x, m, :].astype(F32)
            own = v.b_cb[m, :] - (own + tot(v.b_lxr, m))
            v.b_h[x, c, m, :] = own.astype(BF)

        core = []
        cbs.wait_recv()
        at = pl.ds(pl.multiple_of(c * 512, 128), 512)
        v.b_cb[...] = both(v.i_cb[:, at], v.b_cbs[:, at])
        yield from exchange(
            [
                (d - 1, v.b_k.at[(x + d) % 4], v.b_lr.at[(x + d) % 4], at_x(d))
                for d in (1, 3, 2)
            ],
            v.b_lxs,
            v.b_lxr,
            finish,
            v.b_h.at[x, c],
            [(at_x(d), v.b_h.at[(x + 4 - d) % 4, c]) for d in (1, 3, 2)],
            core,
        )
        need(v.wci)
        arrive(core)
        back_mm(v.wci, 0, v.b_h, 1024, v.b_k)
        got = []
        for d in (1, 3, 2):
            v.b_ms[d - 1] = v.b_k[(z + d) % 4].astype(BF)
            got.append(send(v.b_ms.at[d - 1], v.b_mr.at[d - 1], at_z(d)))
        yield
        arrive(got)

        @tiles(512, 128)
        def _(m):
            v.o_cx[m, :] = v.b_k[z, m, :] + tot(v.b_mr, m)

        emit(v.o_cx, 3)

    chains = dict(B=backward(), F=forward())
    for name in ORDER + "BF" * 60:
        if name in chains:
            try:
                next(chains[name])
            except StopIteration:
                del chains[name]
    for copy in loads.values():
        copy.wait()
    for copy in sent:
        copy.wait_send()
    for copy in stores:
        copy.wait()


def write_out(*refs):
    n = len(OUTPUTS)
    stage, sems = refs[2 * n : 3 * n], refs[3 * n]
    loads = [pltpu.make_async_copy(refs[i], stage[i], sems.at[0, i]) for i in range(n)]
    for copy in loads:
        copy.start()
    stores = [pltpu.make_async_copy(stage[i], refs[n + i], sems.at[1, i]) for i in range(n)]
    for load, store in zip(loads, stores):
        load.wait()
        store.start()
    for store in stores:
        store.wait()


def per_device(*args):
    any_space = pl.BlockSpec(memory_space=pl.ANY)
    shapes = (
        (1, 64, 1024),
        (1, 64, 768),
        (1, 96, 512),
        (1, 512, 128),
        (1, 384, 128),
        (384, 128),
    )
    scratch = [pltpu.VMEM(s, t) for part in (INPUTS, OUTPUTS, SCRATCH) for s, t in part.values()]
    scratch += [
        pltpu.SemaphoreType.DMA((N_REMOTE,)),
        pltpu.SemaphoreType.DMA((N_REMOTE,)),
        pltpu.SemaphoreType.DMA((N_LOCAL,)),
    ]
    args = list(args)
    for i in (10, 11):
        args[i] = jnp.swapaxes(args[i], 1, 2)
    outs = pl.pallas_call(
        body,
        out_shape=tuple(jax.ShapeDtypeStruct(s, F32) for s in shapes),
        in_specs=[any_space] * len(INPUTS),
        out_specs=(any_space,) * len(OUTPUTS),
        scratch_shapes=scratch,
        compiler_params=pltpu.CompilerParams(
            collective_id=0, has_side_effects=True, vmem_limit_bytes=63 * 1024 * 1024
        ),
    )(*args)
    outs = pl.pallas_call(
        write_out,
        out_shape=tuple(jax.ShapeDtypeStruct(s, F32) for s in shapes),
        in_specs=[any_space] * len(OUTPUTS),
        out_specs=(any_space,) * len(OUTPUTS),
        scratch_shapes=[pltpu.VMEM(s, F32) for s in shapes]
        + [pltpu.SemaphoreType.DMA((2, len(OUTPUTS)))],
    )(*outs)
    return tuple(jnp.swapaxes(o, 1, 2) if i < 2 else o for i, o in enumerate(outs))


def solution(mesh):
    return jax.shard_map(
        per_device,
        mesh=mesh,
        in_specs=(
            P("sec", "col", "row"),
            P("sec", "row", "col"),
            P("sec", "col", "row"),
            P("sec", "row", "col"),
            P("col", ("sec", "row")),
            P(),
            P(),
            P("sec", "row", "col"),
            P("sec", "row", "col"),
            P(("sec", "row"), "col"),
            P("sec", "col", "row"),
            P("sec", "col", "row"),
            P("col", ("sec", "row"), None),
        ),
        out_specs=(
            P("sec", "col", "row"),
            P("sec", "col", "row"),
            P("col", ("sec", "row"), None),
            P("sec", "row", "col"),
            P("sec", "row", "col"),
            P(("sec", "row"), "col"),
        ),
        check_vma=False,
    )
```
